32 devices in a mesh: parts: 2 (over x), pop: 8 (over z, y), mp: 2 (over core).
Axes of the slice: x: 2, y: 2, z: 4, core: 2. Of those that a mesh axis runs over, the one named last changes fastest.
Arguments:
- prompt_states: bfloat16 [1024, 8192], P('parts'), parts along dimension 0, may hold values from -6 to 6
- weight_codes: bfloat16 [8192, 16384], P(None, ('pop', 'mp')), may hold values from -448 to 448
- block_scales: float32 [64, 128], P(None, ('pop', 'mp')), may hold values from 2e-05 to 8e-05
- readout: float32 [16384], P(('pop', 'mp')), may hold values from -6 to 6
- noise_rows: bfloat16 [32, 8192], P(('parts', 'pop')), parts along dimension 0, may hold values from -6 to 6
- noise_cols: bfloat16 [32, 16384], P(('parts', 'pop')), parts along dimension 0, may hold values from -6 to 6
- ranks: int32 [64], P('parts'), parts along dimension 0, may hold values from 0 to 31, each once
Outputs:
- direction: bfloat16 [16384, 16384], P('parts', ('pop', 'mp')), parts along dimension 0
- scores: float32 [64], P('parts'), parts along dimension 0
The draws below stay inside these ranges and needn't reach their ends.
There are 2 independent parts, one for each index of `parts`. The reference program is written for one: setup_inputs(seed, part) draws one part's arguments, and reference() takes and returns one part's arrays. A program takes and returns all parts, laid end to end along the dimension named above; an argument that names none is the same for every part. Nothing has to cross between parts.
Inputs may be any that keep to these rules, and one draw needn't show every extreme that they name: `ranks`: every number from 0 to 31 appears exactly once; higher is fitter.
All inputs are finite; a program needn't handle non-finite values.
Results may differ from the reference program's by a relative error of at most 0.0046.
The reference program's roundings to bfloat16 on the way (of `scaled_cols` and `updated`) count: a program that leaves them out, or rounds other values in their place, can miss the bound.
Values may be sent and summed in bfloat16 or wider, within the bound.
No kernel may reach another device: no remote copies, remote signals or barrier semaphores. Data moves between devices by JAX's collectives and lax.ppermute only.
A program may use at most 192 MiB of HBM per device.

```python
import math
import jax
import jax.numpy as jnp
from jax import lax

D = 8192
FF = 16384
BLK = 128
TOK = 512
PAIRS = 16
MEMBERS = 32


def block_scale(rng, shape, cuts, smallest, high):
    factor_of = 1.0
    for position, parts in cuts:
        draws = jax.random.uniform(jax.random.fold_in(jax.random.fold_in(rng, 6), position), (parts,), jnp.float32, smallest / len(cuts), high / len(cuts))
        factor_of = factor_of * jnp.repeat(jnp.exp(draws), shape[position] // parts).reshape((-1,) + (1,) * (len(shape) - 1 - position))
    return factor_of


def scatter_about(key, extent, scale, bound, split=(), dtype=jnp.bfloat16):
    result = jax.random.normal(key, extent, jnp.float32) * scale
    if len(split) > 0:
        result = block_scale(key, extent, split, -0.22, 0.18) * result
    return jnp.clip(result, min=-bound, max=bound).astype(dtype)


def setup_inputs(seed: int = 0, part: int = 0) -> dict:
    arg_keys = jax.random.split(jax.random.key(seed), 8)
    part_splits = jax.random.split(jax.random.fold_in(arg_keys[7], part), 8)
    prompt_states = scatter_about(part_splits[0], (TOK, D), 1.0, 6.0)
    weight_codes = jnp.clip(jax.random.uniform(arg_keys[1], (D, FF), jnp.float32, -448.0, 448.0) * block_scale(arg_keys[1], (D, FF), ((1, 16),), -0.4, 0.0), -448.0, 448.0).astype(jnp.bfloat16)
    block_scales = jnp.clip(jnp.exp(math.log(7.999999797903001e-05) - 1.3862944 * jax.random.uniform(arg_keys[2], (D // BLK, FF // BLK), jnp.float32) ** block_scale(arg_keys[2], (D // BLK, FF // BLK), ((1, 16),), -0.2, 0.2)), 1.9999999494757503e-05, 7.999999797903001e-05)
    readout = scatter_about(arg_keys[3], (FF,), 1.0, 6.0, ((0, 16),), jnp.float32)
    noise_rows = scatter_about(part_splits[4], (PAIRS, D), 1.0, 6.0, ((0, 8),))
    noise_cols = scatter_about(part_splits[5], (PAIRS, FF), 1.0, 6.0, ((0, 8),))
    ranks = jax.random.permutation(part_splits[6], MEMBERS).astype(jnp.int32)
    return {"prompt_states": prompt_states, "weight_codes": weight_codes, "block_scales": block_scales, "readout": readout, "noise_rows": noise_rows, "noise_cols": noise_cols, "ranks": ranks}


SIGMA_NOISE = 0.5
STEP_SIZE = 1.0
pair_group = 8

def member_scores(base, projections, factor_cols, readout):
    tokens = base.shape[0]
    pairs = projections.shape[1]
    width = base.shape[1]
    proj_groups = projections.reshape(tokens, pairs // pair_group, pair_group).transpose(1, 0, 2)
    col_groups = factor_cols.reshape(pairs // pair_group, pair_group, width)
    base_act = jax.nn.silu(base)[:, None, :]

    def one_group(items):
        proj_g, cols_g = items
        offset = SIGMA_NOISE * proj_g[:, :, None] * cols_g[None, :, :]
        plus = lax.optimization_barrier(jnp.sum((jax.nn.silu(base[:, None, :] + offset) - base_act) * readout, axis=(0, 2)))
        minus = lax.optimization_barrier(jnp.sum((jax.nn.silu(base[:, None, :] - offset) - base_act) * readout, axis=(0, 2)))
        return (plus, minus)
    plus, minus = lax.map(one_group, (proj_groups, col_groups))
    return jnp.concatenate([plus.reshape(pairs), minus.reshape(pairs)])

def dequantize_add(codes, scales, direction):
    rows, width = codes.shape
    blocks = codes.astype(jnp.float32).reshape(rows // BLK, BLK, width // BLK, BLK) * scales[:, None, :, None]
    summed = blocks.reshape(rows, width) + STEP_SIZE / math.sqrt(rows) * direction.astype(jnp.float32)
    return summed.astype(jnp.bfloat16)

def reference(prompt_states, weight_codes, block_scales, readout, noise_rows, noise_cols, ranks):
    rank_vals = ranks.astype(jnp.float32)
    pair_weight = (rank_vals[:PAIRS] - rank_vals[PAIRS:]) / (MEMBERS - 1)
    scaled_cols = (pair_weight[:, None] * noise_cols.astype(jnp.float32) * (1.0 / math.sqrt(PAIRS))).astype(jnp.bfloat16)
    direction = jnp.dot(noise_rows.T, scaled_cols, preferred_element_type=jnp.float32).astype(jnp.bfloat16)
    updated = dequantize_add(weight_codes, block_scales, direction)
    base = jnp.dot(prompt_states, updated, preferred_element_type=jnp.float32)
    projections = jnp.dot(prompt_states, noise_rows.T, preferred_element_type=jnp.float32) * (1.0 / math.sqrt(D))
    partial_sums = member_scores(base, projections, noise_cols.astype(jnp.float32), readout)
    scores = partial_sums * (1.0 / math.sqrt(TOK * FF))
    return (direction, scores)
```

```python
import math

import jax
import jax.numpy as jnp
from jax import lax
from jax.experimental import pallas as pl
from jax.experimental.pallas import tpu as pltpu
from jax.sharding import PartitionSpec as P

FF = 16384
BLK = 128
TOK = 512
SIGMA_NOISE = 0.5
STEP_SIZE = 1.0
MIB = 1 << 20


def code_base_kernel(scales_ref, states_ref, codes_ref, out_ref):
    depth, tile = codes_ref.shape
    first = pl.program_id(0) * (tile // BLK)
    rows = []
    for kb in range(depth // BLK):
        cols = []
        for cb in range(tile // BLK):
            block = codes_ref[kb * BLK : (kb + 1) * BLK, cb * BLK : (cb + 1) * BLK]
            scaled = block.astype(jnp.float32) * scales_ref[first + cb, kb]
            cols.append(scaled.astype(jnp.bfloat16))
        rows.append(jnp.concatenate(cols, axis=1) if len(cols) > 1 else cols[0])
    weights = jnp.concatenate(rows, axis=0)
    out_ref[...] = jnp.dot(states_ref[...], weights, preferred_element_type=jnp.float32)


def code_base(states, codes, scales_t):
    tokens, depth = states.shape
    width = codes.shape[1]
    tile = min(256, width)
    return pl.pallas_call(
        code_base_kernel,
        grid=(width // tile,),
        in_specs=[
            pl.BlockSpec(memory_space=pltpu.SMEM),
            pl.BlockSpec(memory_space=pltpu.VMEM),
            pl.BlockSpec((depth, tile), lambda j: (0, j)),
        ],
        out_specs=pl.BlockSpec((tokens, tile), lambda j: (0, j)),
        out_shape=jax.ShapeDtypeStruct((tokens, width), jnp.float32),
        compiler_params=pltpu.CompilerParams(vmem_limit_bytes=28 * MIB),
        cost_estimate=pl.CostEstimate(
            flops=2 * tokens * depth * width,
            bytes_accessed=2 * depth * width + 4 * tokens * width,
            transcendentals=0,
        ),
        name="code_base",
    )(scales_t, states, codes)


def split3(value):
    hi = value.astype(jnp.bfloat16)
    rest = value - hi.astype(jnp.float32)
    mid = rest.astype(jnp.bfloat16)
    low = (rest - mid.astype(jnp.float32)).astype(jnp.bfloat16)
    return hi, mid, low


def score_kernel(
    states_ref, rows_ref, base_ref, cols_ref, scaled_ref, readout_ref, out_ref,
    half_ref, split_ref, factor_ref, terms_ref,
):
    tokens, width = base_ref.shape
    pairs, depth = rows_ref.shape
    proj = lax.dot_general(
        states_ref[...], rows_ref[...], (((1,), (1,)), ((), ())),
        preferred_element_type=jnp.float32,
    ) * (1.0 / math.sqrt(depth))
    split_ref[...] = jnp.concatenate(split3(proj), axis=1)
    scaled = scaled_ref[...]
    step = jnp.dot(
        split_ref[...], jnp.concatenate([scaled, scaled, scaled], axis=0),
        preferred_element_type=jnp.float32,
    )
    half_ref[...] = (base_ref[...] + STEP_SIZE * step) * 0.5

    def rest_step(i, acc):
        u = half_ref[pl.ds(pl.multiple_of(i * 8, 8), 8), :]
        return acc + u * jnp.tanh(u)

    rest = lax.fori_loop(0, tokens // 8, rest_step, jnp.zeros((8, width), jnp.float32))
    rest = jnp.sum(rest, axis=0, keepdims=True)
    readout = readout_ref[...]

    def one_pair(p, carry):
        which = lax.broadcasted_iota(jnp.int32, (3 * pairs, 128), 0)
        hit = (which == p) | (which == p + pairs) | (which == p + 2 * pairs)
        pick = jnp.where(hit, 0.5 * SIGMA_NOISE, 0.0).astype(jnp.bfloat16)
        factor_ref[...] = jnp.dot(split_ref[...], pick, preferred_element_type=jnp.float32)
        col = jnp.broadcast_to(cols_ref[pl.ds(p, 1), :], (8, width))

        def step(i, acc):
            plus, minus, total = acc
            rows = pl.ds(pl.multiple_of(i * 8, 8), 8)
            factor = factor_ref[rows, :]
            u = half_ref[rows, :]
            shift = jnp.concatenate([factor] * (width // 128), axis=1) * col
            up = u + shift
            um = u - shift
            return plus + up * jnp.tanh(up), minus + um * jnp.tanh(um), total + factor

        zero = jnp.zeros((8, width), jnp.float32)
        plus, minus, total = lax.fori_loop(
            0, tokens // 8, step, (zero, zero, jnp.zeros((8, 128), jnp.float32)), unroll=4
        )
        total = jnp.sum(total, axis=0, keepdims=True)
        linear = jnp.concatenate([total] * (width // 128), axis=1) * cols_ref[pl.ds(p, 1), :]
        plus = jnp.sum(plus, axis=0, keepdims=True)
        minus = jnp.sum(minus, axis=0, keepdims=True)
        terms_ref[pl.ds(p, 1), :] = (plus - rest + linear) * readout
        terms_ref[pl.ds(p + pairs, 1), :] = (minus - rest - linear) * readout
        return carry

    lax.fori_loop(0, pairs, one_pair, 0)
    lanes = terms_ref[:, 0:128]
    for j in range(1, width // 128):
        lanes = lanes + terms_ref[:, j * 128 : (j + 1) * 128]
    sums = jnp.sum(lanes.T, axis=0, keepdims=True)
    out_ref[...] = jnp.broadcast_to(sums, out_ref.shape)


def score_sums(states, rows, base, cols, scaled, readout, copies):
    tokens, width = base.shape
    pairs = rows.shape[0]
    vmem = pl.BlockSpec(memory_space=pltpu.VMEM)
    return pl.pallas_call(
        score_kernel,
        in_specs=[vmem] * 6,
        out_specs=vmem,
        out_shape=jax.ShapeDtypeStruct((copies, 2 * pairs), jnp.float32),
        scratch_shapes=[
            pltpu.VMEM((tokens, width), jnp.float32),
            pltpu.VMEM((tokens, 3 * pairs), jnp.bfloat16),
            pltpu.VMEM((tokens, 128), jnp.float32),
            pltpu.VMEM((2 * pairs, width), jnp.float32),
        ],
        compiler_params=pltpu.CompilerParams(vmem_limit_bytes=20 * MIB),
        cost_estimate=pl.CostEstimate(
            flops=14 * tokens * width * pairs,
            bytes_accessed=4 * tokens * width,
            transcendentals=2 * tokens * width * pairs,
        ),
        name="score_sums",
    )(states, rows, base, cols, scaled, readout)


def direction_kernel(rows_ref, scaled_ref, out_ref):
    out_ref[...] = lax.dot_general(
        rows_ref[...], scaled_ref[...], (((0,), (0,)), ((), ())),
        preferred_element_type=jnp.float32,
    ).astype(jnp.bfloat16)


def make_direction(rows, scaled):
    pairs, depth = rows.shape
    width = scaled.shape[1]
    block = 1024
    return pl.pallas_call(
        direction_kernel,
        grid=(depth // block,),
        in_specs=[
            pl.BlockSpec((pairs, block), lambda i: (0, i)),
            pl.BlockSpec((pairs, width), lambda i: (0, 0)),
        ],
        out_specs=pl.BlockSpec((block, width), lambda i: (i, 0)),
        out_shape=jax.ShapeDtypeStruct((depth, width), jnp.bfloat16),
        compiler_params=pltpu.CompilerParams(vmem_limit_bytes=20 * MIB),
        cost_estimate=pl.CostEstimate(
            flops=2 * pairs * depth * width, bytes_accessed=2 * depth * width, transcendentals=0
        ),
        name="direction",
    )(rows, scaled)


def solution(mesh):
    pop, mp = mesh.shape["pop"], mesh.shape["mp"]

    def per_device(prompt_states, weight_codes, block_scales, readout, noise_rows, noise_cols, ranks):
        depth, width = weight_codes.shape
        own = noise_rows.shape[0]
        pairs = own * pop
        members = ranks.shape[0]
        core = lax.axis_index("mp")
        my_cols = lax.dynamic_index_in_dim(
            noise_cols.reshape(own, pop, mp, width), core, 2, keepdims=False
        ).transpose(1, 0, 2)
        parcel = jnp.concatenate(
            [jnp.broadcast_to(noise_rows[None], (pop, own, depth)), my_cols], axis=2
        )
        arrived = lax.all_to_all(parcel, "pop", split_axis=0, concat_axis=0, tiled=True)
        arrived = arrived.reshape(pairs, depth + width)

        base = code_base(prompt_states, weight_codes, block_scales.T)

        rows = arrived[:, :depth]
        cols = arrived[:, depth:].astype(jnp.float32)
        rank_vals = ranks.astype(jnp.float32)
        pair_weight = (rank_vals[:pairs] - rank_vals[pairs:]) / (members - 1)
        scaled = (pair_weight[:, None] * cols * (1.0 / math.sqrt(pairs))).astype(jnp.bfloat16)
        sums = score_sums(
            prompt_states, rows, base, cols, scaled, readout[None, :], pop * mp
        )
        everyone = lax.all_to_all(
            sums[:, None, :], ("pop", "mp"), split_axis=0, concat_axis=0, tiled=True
        )
        direction = make_direction(rows, scaled)
        scores = jnp.sum(everyone, axis=(0, 1)) * (1.0 / math.sqrt(TOK * FF))
        return (direction, scores)

    in_specs = (
        P("parts", None),
        P(None, ("pop", "mp")),
        P(None, ("pop", "mp")),
        P(("pop", "mp")),
        P(("parts", "pop"), None),
        P(("parts", "pop"), None),
        P("parts"),
    )
    out_specs = (P("parts", ("pop", "mp")), P("parts"))
    return jax.shard_map(
        per_device, mesh=mesh, in_specs=in_specs, out_specs=out_specs, check_vma=False
    )
```

```python
import math

import jax
import jax.numpy as jnp
from jax import lax
from jax.experimental import pallas as pl
from jax.experimental.pallas import tpu as pltpu
from jax.sharding import PartitionSpec as P

FF = 16384
BLK = 128
TOK = 512
SIGMA_NOISE = 0.5
STEP_SIZE = 1.0
MIB = 1 << 20


def split3(value):
    hi = value.astype(jnp.bfloat16)
    rest = value - hi.astype(jnp.float32)
    mid = rest.astype(jnp.bfloat16)
    low = (rest - mid.astype(jnp.float32)).astype(jnp.bfloat16)
    return hi, mid, low


def parcel_kernel(
    states_hbm, rows_hbm, cols_hbm, out_ref, states_ref, rows_ref, cols_ref, proj_ref,
    sems, row_sem, col_sem,
):
    pop, own, total = out_ref.shape
    tokens, depth = states_ref.shape
    width = total - depth - 3 * tokens
    cores = cols_ref.shape[1] // (pop * width)
    core = lax.axis_index("mp")
    count = sems.shape[0]
    chunk = depth // count
    ahead = 2

    def state_copy(k):
        span = pl.ds(pl.multiple_of(k * chunk, chunk), chunk)
        return pltpu.make_async_copy(states_hbm.at[:, span], states_ref.at[:, span], sems.at[k])

    row_copy = pltpu.make_async_copy(rows_hbm, rows_ref, row_sem)
    col_copy = pltpu.make_async_copy(cols_hbm, cols_ref, col_sem)
    row_copy.start()
    col_copy.start()
    for k in range(ahead):
        state_copy(k).start()
    row_copy.wait()
    col_copy.wait()
    rows = rows_ref[...]
    for dest in range(pop):
        out_ref[dest, :, :depth] = rows
        start = pl.multiple_of((dest * cores + core) * width, width)
        out_ref[dest, :, depth : depth + width] = cols_ref[:, pl.ds(start, width)]
    proj_ref[...] = jnp.zeros_like(proj_ref)

    @pl.loop(0, count)
    def _(k):
        state_copy(k).wait()

        @pl.when(k + ahead < count)
        def _():
            state_copy(k + ahead).start()

        span = pl.ds(pl.multiple_of(k * chunk, chunk), chunk)
        proj_ref[...] += lax.dot_general(
            states_ref[:, span], rows_ref[:, span], (((1,), (1,)), ((), ())),
            preferred_element_type=jnp.float32,
        )

    proj = proj_ref[...]
    proj = proj.T * (1.0 / math.sqrt(depth))
    parts = jnp.concatenate(split3(proj), axis=1)
    for dest in range(pop):
        out_ref[dest, :, depth + width :] = parts


def make_parcel(states, rows, cols, pop, width):
    own, depth = rows.shape
    tokens = states.shape[0]
    count = 4
    return pl.pallas_call(
        parcel_kernel,
        in_specs=[pl.BlockSpec(memory_space=pltpu.HBM)] * 3,
        out_specs=pl.BlockSpec(memory_space=pltpu.VMEM),
        out_shape=jax.ShapeDtypeStruct((pop, own, depth + width + 3 * tokens), jnp.bfloat16),
        scratch_shapes=[
            pltpu.VMEM((tokens, depth), jnp.bfloat16),
            pltpu.VMEM(rows.shape, jnp.bfloat16),
            pltpu.VMEM(cols.shape, jnp.bfloat16),
            pltpu.VMEM((tokens, own), jnp.float32),
            pltpu.SemaphoreType.DMA((count,)),
            pltpu.SemaphoreType.DMA,
            pltpu.SemaphoreType.DMA,
        ],
        compiler_params=pltpu.CompilerParams(vmem_limit_bytes=60 * MIB),
        name="parcel",
    )(states, rows, cols)


def code_base_kernel(
    scales_hbm, states_hbm, codes_hbm, out_ref, states_ref, codes_ref, scales_ref,
    scale_sem, state_sems, code_sems,
):
    depth, width = codes_ref.shape
    count = state_sems.shape[0]
    chunk = depth // count
    ahead = 3

    def copies(k):
        span = pl.ds(k * chunk, chunk)
        return (
            pltpu.make_async_copy(states_hbm.at[:, span], states_ref.at[:, span], state_sems.at[k]),
            pltpu.make_async_copy(codes_hbm.at[span, :], codes_ref.at[span, :], code_sems.at[k]),
        )

    scale_copy = pltpu.make_async_copy(scales_hbm, scales_ref, scale_sem)
    scale_copy.start()
    for k in range(min(ahead, count)):
        for copy in copies(k):
            copy.start()
    scale_copy.wait()
    for k in range(count):
        if k + ahead < count:
            for copy in copies(k + ahead):
                copy.start()
        for copy in copies(k):
            copy.wait()
        rows = []
        for i in range(k * chunk, (k + 1) * chunk, BLK):
            cols = []
            for c in range(0, width, BLK):
                block = codes_ref[i : i + BLK, c : c + BLK].astype(jnp.float32)
                cols.append((block * scales_ref[c // BLK, i // BLK]).astype(jnp.bfloat16))
            rows.append(jnp.concatenate(cols, axis=1) if len(cols) > 1 else cols[0])
        weights = jnp.concatenate(rows, axis=0)
        part = jnp.dot(
            states_ref[:, k * chunk : (k + 1) * chunk], weights,
            preferred_element_type=jnp.float32,
        )
        if k == 0:
            out_ref[...] = part
        else:
            out_ref[...] += part


def code_base(states, codes, scales_t):
    tokens, depth = states.shape
    width = codes.shape[1]
    count = 8
    vmem = pl.BlockSpec(memory_space=pltpu.VMEM)
    away = pl.BlockSpec(memory_space=pltpu.HBM)
    return pl.pallas_call(
        code_base_kernel,
        in_specs=[away, away, away],
        out_specs=vmem,
        out_shape=jax.ShapeDtypeStruct((tokens, width), jnp.float32),
        scratch_shapes=[
            pltpu.VMEM((tokens, depth), jnp.bfloat16),
            pltpu.VMEM((depth, width), jnp.bfloat16),
            pltpu.SMEM(scales_t.shape, jnp.float32),
            pltpu.SemaphoreType.DMA,
            pltpu.SemaphoreType.DMA((count,)),
            pltpu.SemaphoreType.DMA((count,)),
        ],
        compiler_params=pltpu.CompilerParams(vmem_limit_bytes=48 * MIB),
        cost_estimate=pl.CostEstimate(
            flops=2 * tokens * depth * width,
            bytes_accessed=2 * depth * (tokens + width),
            transcendentals=0,
        ),
        name="code_base",
    )(scales_t, states, codes)


def score_kernel(
    ranks_ref, split_ref, base_ref, cols_ref, readout_ref, out_ref, scaled_ref,
    half_ref, factor_ref, terms_ref,
):
    tokens, width = base_ref.shape
    pairs = cols_ref.shape[0]
    split = jnp.concatenate(
        [split_ref[:, i * tokens : (i + 1) * tokens] for i in range(3)], axis=0
    )
    over_pairs = (((0,), (0,)), ((), ()))
    which = lax.broadcasted_iota(jnp.int32, (pairs, 128), 0)
    gap = jnp.zeros((pairs, 128), jnp.float32)
    for q in range(pairs):
        mine = (ranks_ref[q] - ranks_ref[q + pairs]).astype(jnp.float32)
        gap = jnp.where(which == q, mine, gap)
    pair_weight = gap / (2 * pairs - 1)
    scaled = (
        jnp.concatenate([pair_weight] * (width // 128), axis=1)
        * cols_ref[...] * (1.0 / math.sqrt(pairs))
    ).astype(jnp.bfloat16)
    scaled_ref[...] = scaled
    step = lax.dot_general(
        split, jnp.concatenate([scaled, scaled, scaled], axis=0), over_pairs,
        preferred_element_type=jnp.float32,
    )
    half_ref[...] = (base_ref[...] + STEP_SIZE * step) * 0.5

    def rest_step(i, acc):
        u = half_ref[pl.ds(pl.multiple_of(i * 8, 8), 8), :]
        return acc + u * jnp.tanh(u)

    rest = lax.fori_loop(
        0, tokens // 8, rest_step, jnp.zeros((8, width), jnp.float32), unroll=8
    )
    rest = jnp.sum(rest, axis=0, keepdims=True)
    readout = readout_ref[...]

    for q in range(pairs):
        which = lax.broadcasted_iota(jnp.int32, (3 * pairs, 128), 0)
        hit = (which == q) | (which == q + pairs) | (which == q + 2 * pairs)
        pick = jnp.where(hit, 0.5 * SIGMA_NOISE, 0.0).astype(jnp.bfloat16)
        factor_ref[q] = lax.dot_general(
            split, pick, over_pairs, preferred_element_type=jnp.float32
        )

    def one_pair(p, carry):
        col = jnp.broadcast_to(cols_ref[pl.ds(p, 1), :], (8, width))

        def step(i, acc):
            plus, minus, total = acc
            rows = pl.ds(pl.multiple_of(i * 8, 8), 8)
            factor = factor_ref[p, rows, :]
            u = half_ref[rows, :]
            shift = jnp.concatenate([factor] * (width // 128), axis=1) * col
            up = u + shift
            um = u - shift
            return plus + up * jnp.tanh(up), minus + um * jnp.tanh(um), total + factor

        zero = jnp.zeros((8, width), jnp.float32)
        plus, minus, total = lax.fori_loop(
            0, tokens // 8, step, (zero, zero, jnp.zeros((8, 128), jnp.float32)), unroll=16
        )
        total = jnp.sum(total, axis=0, keepdims=True)
        linear = jnp.concatenate([total] * (width // 128), axis=1) * cols_ref[pl.ds(p, 1), :]
        plus = jnp.sum(plus, axis=0, keepdims=True)
        minus = jnp.sum(minus, axis=0, keepdims=True)
        terms_ref[pl.ds(p, 1), :] = (plus - rest + linear) * readout
        terms_ref[pl.ds(p + pairs, 1), :] = (minus - rest - linear) * readout
        return carry

    lax.fori_loop(0, pairs, one_pair, 0)
    lanes = terms_ref[:, 0:128]
    for j in range(1, width // 128):
        lanes = lanes + terms_ref[:, j * 128 : (j + 1) * 128]
    sums = jnp.sum(lanes.T, axis=0, keepdims=True)
    out_ref[...] = jnp.broadcast_to(sums, out_ref.shape)


def score_sums(ranks, split, base, cols, readout, copies):
    tokens, width = base.shape
    pairs = cols.shape[0]
    vmem = pl.BlockSpec(memory_space=pltpu.VMEM)
    return pl.pallas_call(
        score_kernel,
        in_specs=[pl.BlockSpec(memory_space=pltpu.SMEM), vmem, vmem, vmem, vmem],
        out_specs=(vmem, vmem),
        out_shape=(
            jax.ShapeDtypeStruct((copies, 2 * pairs), jnp.float32),
            jax.ShapeDtypeStruct((pairs, width), jnp.bfloat16),
        ),
        scratch_shapes=[
            pltpu.VMEM((tokens, width), jnp.float32),
            pltpu.VMEM((pairs, tokens, 128), jnp.float32),
            pltpu.VMEM((2 * pairs, width), jnp.float32),
        ],
        compiler_params=pltpu.CompilerParams(
            vmem_limit_bytes=16 * MIB + 512 * pairs * tokens
        ),
        cost_estimate=pl.CostEstimate(
            flops=14 * tokens * width * pairs,
            bytes_accessed=4 * tokens * width,
            transcendentals=2 * tokens * width * pairs,
        ),
        name="score_sums",
    )(ranks, split, base, cols, readout)


def direction_kernel(rows_ref, scaled_ref, out_ref):
    out_ref[...] = lax.dot_general(
        rows_ref[...], scaled_ref[...], (((0,), (0,)), ((), ())),
        preferred_element_type=jnp.float32,
    ).astype(jnp.bfloat16)


def make_direction(rows, scaled):
    pairs, depth = rows.shape
    width = scaled.shape[1]
    block = 2048
    return pl.pallas_call(
        direction_kernel,
        grid=(depth // block,),
        in_specs=[
            pl.BlockSpec((pairs, block), lambda i: (0, i)),
            pl.BlockSpec((pairs, width), lambda i: (0, 0)),
        ],
        out_specs=pl.BlockSpec((block, width), lambda i: (i, 0)),
        out_shape=jax.ShapeDtypeStruct((depth, width), jnp.bfloat16),
        compiler_params=pltpu.CompilerParams(vmem_limit_bytes=20 * MIB),
        cost_estimate=pl.CostEstimate(
            flops=2 * pairs * depth * width, bytes_accessed=2 * depth * width, transcendentals=0
        ),
        name="direction",
    )(rows, scaled)


def solution(mesh):
    pop, mp = mesh.shape["pop"], mesh.shape["mp"]

    def per_device(prompt_states, weight_codes, block_scales, readout, noise_rows, noise_cols, ranks):
        depth, width = weight_codes.shape
        own = noise_rows.shape[0]
        pairs = own * pop
        parcel = make_parcel(prompt_states, noise_rows, noise_cols, pop, width)
        arrived = lax.all_to_all(parcel, "pop", split_axis=0, concat_axis=0, tiled=True)
        arrived = arrived.reshape(pairs, parcel.shape[2])

        base = code_base(prompt_states, weight_codes, block_scales.T)

        rows = arrived[:, :depth]
        cols = arrived[:, depth : depth + width].astype(jnp.float32)
        split = arrived[:, depth + width :]
        sums, scaled = score_sums(ranks, split, base, cols, readout[None, :], pop * mp)
        everyone = lax.all_to_all(
            sums[:, None, :], ("pop", "mp"), split_axis=0, concat_axis=0, tiled=True
        )
        direction = make_direction(rows, scaled)
        scores = jnp.sum(everyone, axis=(0, 1)) * (1.0 / math.sqrt(TOK * FF))
        return (direction, scores)

    in_specs = (
        P("parts", None),
        P(None, ("pop", "mp")),
        P(None, ("pop", "mp")),
        P(("pop", "mp")),
        P(("parts", "pop"), None),
        P(("parts", "pop"), None),
        P("parts"),
    )
    out_specs = (P("parts", ("pop", "mp")), P("parts"))
    return jax.shard_map(
        per_device, mesh=mesh, in_specs=in_specs, out_specs=out_specs, check_vma=False
    )
```

```python
import math

import jax
import jax.numpy as jnp
from jax import lax
from jax.experimental import pallas as pl
from jax.experimental.pallas import tpu as pltpu
from jax.sharding import PartitionSpec as P

FF = 16384
BLK = 128
TOK = 512
SIGMA_NOISE = 0.5
STEP_SIZE = 1.0
MIB = 1 << 20


def split3(value):
    hi = value.astype(jnp.bfloat16)
    rest = value - hi.astype(jnp.float32)
    mid = rest.astype(jnp.bfloat16)
    low = (rest - mid.astype(jnp.float32)).astype(jnp.bfloat16)
    return hi, mid, low


def parcel_kernel(
    states_hbm, rows_hbm, cols_hbm, out_ref, states_ref, rows_ref, cols_ref, proj_ref,
    sems, row_sem, col_sem,
):
    members, own, total = out_ref.shape
    share, depth = states_ref.shape
    width = cols_ref.shape[1] // members
    depth_share = total - width - 3 * share
    core = lax.axis_index("mp")
    first_token = pl.multiple_of(core * share, share)
    first_row = pl.multiple_of(core * depth_share, depth_share)
    count = sems.shape[0]
    chunk = depth // count
    ahead = 2

    def state_copy(k):
        span = pl.ds(pl.multiple_of(k * chunk, chunk), chunk)
        return pltpu.make_async_copy(
            states_hbm.at[pl.ds(first_token, share), span], states_ref.at[:, span], sems.at[k]
        )

    row_copy = pltpu.make_async_copy(rows_hbm, rows_ref, row_sem)
    col_copy = pltpu.make_async_copy(cols_hbm, cols_ref, col_sem)
    row_copy.start()
    col_copy.start()
    for k in range(ahead):
        state_copy(k).start()
    row_copy.wait()
    col_copy.wait()
    rows = rows_ref[:, pl.ds(first_row, depth_share)]
    for dest in range(members):
        out_ref[dest, :, :depth_share] = rows
        out_ref[dest, :, depth_share : depth_share + width] = cols_ref[
            :, dest * width : (dest + 1) * width
        ]
    proj_ref[...] = jnp.zeros_like(proj_ref)

    @pl.loop(0, count)
    def _(k):
        state_copy(k).wait()

        @pl.when(k + ahead < count)
        def _():
            state_copy(k + ahead).start()

        span = pl.ds(pl.multiple_of(k * chunk, chunk), chunk)
        proj_ref[...] += lax.dot_general(
            states_ref[:, span], rows_ref[:, span], (((1,), (1,)), ((), ())),
            preferred_element_type=jnp.float32,
        )

    proj = proj_ref[...].T * (1.0 / math.sqrt(depth))
    parts = jnp.concatenate(split3(proj), axis=1)
    for dest in range(members):
        out_ref[dest, :, depth_share + width :] = parts


def make_parcel(states, rows, cols, members, cores):
    own, depth = rows.shape
    tokens = states.shape[0]
    width = cols.shape[1] // members
    share = tokens // cores
    count = 4
    return pl.pallas_call(
        parcel_kernel,
        in_specs=[pl.BlockSpec(memory_space=pltpu.HBM)] * 3,
        out_specs=pl.BlockSpec(memory_space=pltpu.VMEM),
        out_shape=jax.ShapeDtypeStruct(
            (members, own, depth // cores + width + 3 * share), jnp.bfloat16
        ),
        scratch_shapes=[
            pltpu.VMEM((share, depth), jnp.bfloat16),
            pltpu.VMEM(rows.shape, jnp.bfloat16),
            pltpu.VMEM(cols.shape, jnp.bfloat16),
            pltpu.VMEM((share, own), jnp.float32),
            pltpu.SemaphoreType.DMA((count,)),
            pltpu.SemaphoreType.DMA,
            pltpu.SemaphoreType.DMA,
        ],
        compiler_params=pltpu.CompilerParams(vmem_limit_bytes=60 * MIB),
        name="parcel",
    )(states, rows, cols)


def code_base_kernel(
    scales_hbm, states_hbm, codes_hbm, out_ref, states_ref, codes_ref, scales_ref,
    scale_sem, state_sems, code_sems,
):
    depth, width = codes_ref.shape
    cuts = chunk_cuts(depth)
    count = len(cuts) - 1
    ahead = 3

    def copies(k):
        span = pl.ds(cuts[k], cuts[k + 1] - cuts[k])
        return (
            pltpu.make_async_copy(states_hbm.at[:, span], states_ref.at[:, span], state_sems.at[k]),
            pltpu.make_async_copy(codes_hbm.at[span, :], codes_ref.at[span, :], code_sems.at[k]),
        )

    scale_copy = pltpu.make_async_copy(scales_hbm, scales_ref, scale_sem)
    scale_copy.start()
    for k in range(min(ahead, count)):
        for copy in copies(k):
            copy.start()
    scale_copy.wait()
    for k in range(count):
        if k + ahead < count:
            for copy in copies(k + ahead):
                copy.start()
        for copy in copies(k):
            copy.wait()
        rows = []
        for i in range(cuts[k], cuts[k + 1], BLK):
            cols = []
            for c in range(0, width, BLK):
                block = codes_ref[i : i + BLK, c : c + BLK].astype(jnp.float32)
                cols.append((block * scales_ref[c // BLK, i // BLK]).astype(jnp.bfloat16))
            rows.append(jnp.concatenate(cols, axis=1) if len(cols) > 1 else cols[0])
        weights = jnp.concatenate(rows, axis=0)
        part = jnp.dot(
            states_ref[:, cuts[k] : cuts[k + 1]], weights, preferred_element_type=jnp.float32
        )
        if k == 0:
            out_ref[...] = part
        else:
            out_ref[...] += part


def chunk_cuts(depth):
    unit = depth // 32
    cuts = [0]
    for size in (1, 3) + (4,) * 7:
        cuts.append(cuts[-1] + size * unit)
    return cuts


def code_base(states, codes, scales_t):
    tokens, depth = states.shape
    width = codes.shape[1]
    count = len(chunk_cuts(depth)) - 1
    vmem = pl.BlockSpec(memory_space=pltpu.VMEM)
    away = pl.BlockSpec(memory_space=pltpu.HBM)
    return pl.pallas_call(
        code_base_kernel,
        in_specs=[away, away, away],
        out_specs=vmem,
        out_shape=jax.ShapeDtypeStruct((tokens, width), jnp.float32),
        scratch_shapes=[
            pltpu.VMEM((tokens, depth), jnp.bfloat16),
            pltpu.VMEM((depth, width), jnp.bfloat16),
            pltpu.SMEM(scales_t.shape, jnp.float32),
            pltpu.SemaphoreType.DMA,
            pltpu.SemaphoreType.DMA((count,)),
            pltpu.SemaphoreType.DMA((count,)),
        ],
        compiler_params=pltpu.CompilerParams(vmem_limit_bytes=48 * MIB),
        cost_estimate=pl.CostEstimate(
            flops=2 * tokens * depth * width,
            bytes_accessed=2 * depth * (tokens + width),
            transcendentals=0,
        ),
        name="code_base",
    )(scales_t, states, codes)


def score_kernel(
    ranks_ref, arrived_ref, base_ref, readout_ref, out_ref, scaled_ref,
    half_ref, cols_ref, factor_ref, terms_ref,
):
    tokens, width = base_ref.shape
    cores, pairs, total = arrived_ref.shape
    share = tokens // cores
    depth_share = total - width - 3 * share
    cols_ref[...] = arrived_ref[0, :, depth_share : depth_share + width].astype(jnp.float32)
    parts = []
    for i in range(3):
        start = depth_share + width + i * share
        parts.append(
            jnp.concatenate(
                [arrived_ref[k, :, start : start + share] for k in range(cores)], axis=1
            )
        )
    split = jnp.concatenate(parts, axis=0)
    over_pairs = (((0,), (0,)), ((), ()))
    which = lax.broadcasted_iota(jnp.int32, (pairs, 128), 0)
    gap = jnp.zeros((pairs, 128), jnp.float32)
    for q in range(pairs):
        mine = (ranks_ref[q] - ranks_ref[q + pairs]).astype(jnp.float32)
        gap = jnp.where(which == q, mine, gap)
    pair_weight = gap / (2 * pairs - 1)
    scaled = (
        jnp.concatenate([pair_weight] * (width // 128), axis=1)
        * cols_ref[...] * (1.0 / math.sqrt(pairs))
    ).astype(jnp.bfloat16)
    scaled_ref[...] = scaled
    step = lax.dot_general(
        split, jnp.concatenate([scaled, scaled, scaled], axis=0), over_pairs,
        preferred_element_type=jnp.float32,
    )
    half_ref[...] = (base_ref[...] + STEP_SIZE * step) * 0.5
    group = min(pairs, 16)
    for first in range(0, pairs, group):
        at = lax.broadcasted_iota(jnp.int32, (3 * pairs, group * 128), 0)
        lane = lax.broadcasted_iota(jnp.int32, (3 * pairs, group * 128), 1)
        goal = first + lane // 128
        hit = (at == goal) | (at == goal + pairs) | (at == goal + 2 * pairs)
        pick = jnp.where(hit, 0.5 * SIGMA_NOISE, 0.0).astype(jnp.bfloat16)
        factor_ref[:, first * 128 : (first + group) * 128] = lax.dot_general(
            split, pick, over_pairs, preferred_element_type=jnp.float32
        )

    tile = min(512, width)
    zero = jnp.zeros((8, tile), jnp.float32)

    def eight(i):
        return pl.ds(pl.multiple_of(i * 8, 8), 8)

    def fold(value):
        lanes = value[:, 0:128]
        for j in range(1, tile // 128):
            lanes = lanes + value[:, j * 128 : (j + 1) * 128]
        return lanes

    for start in range(0, width, tile):
        span = slice(start, start + tile)
        readout = jnp.broadcast_to(readout_ref[:, span], (8, tile))

        def rest_step(i, acc):
            u = half_ref[eight(i), span]
            return acc + u * jnp.tanh(u)

        rest = lax.fori_loop(0, tokens // 8, rest_step, zero, unroll=16)

        def one_pair(p, carry):
            col = jnp.broadcast_to(cols_ref[pl.ds(p, 1), span], (8, tile))
            lanes = pl.ds(pl.multiple_of(p * 128, 128), 128)

            def step(i, acc):
                plus, minus, total = acc
                factor = factor_ref[eight(i), lanes]
                u = half_ref[eight(i), span]
                shift = jnp.concatenate([factor] * (tile // 128), axis=1) * col
                up = u + shift
                um = u - shift
                return plus + up * jnp.tanh(up), minus + um * jnp.tanh(um), total + factor

            plus, minus, total = lax.fori_loop(
                0, tokens // 8, step, (zero, zero, jnp.zeros((8, 128), jnp.float32)),
                unroll=32,
            )
            linear = col * jnp.concatenate([total] * (tile // 128), axis=1)
            plus = fold((plus - rest + linear) * readout)
            minus = fold((minus - rest - linear) * readout)
            if start > 0:
                plus += terms_ref[eight(p), :]
                minus += terms_ref[eight(p + pairs), :]
            terms_ref[eight(p), :] = plus
            terms_ref[eight(p + pairs), :] = minus
            return carry

        lax.fori_loop(0, pairs, one_pair, 0)
    sums = jnp.sum(terms_ref[...].reshape(2 * pairs, 8, 128), axis=1)
    sums = jnp.sum(sums.T, axis=0, keepdims=True)
    out_ref[...] = jnp.broadcast_to(sums, out_ref.shape)


def score_sums(ranks, arrived, base, readout, copies):
    tokens, width = base.shape
    pairs = arrived.shape[1]
    vmem = pl.BlockSpec(memory_space=pltpu.VMEM)
    return pl.pallas_call(
        score_kernel,
        in_specs=[pl.BlockSpec(memory_space=pltpu.SMEM), vmem, vmem, vmem],
        out_specs=(vmem, vmem),
        out_shape=(
            jax.ShapeDtypeStruct((copies, 2 * pairs), jnp.float32),
            jax.ShapeDtypeStruct((pairs, width), jnp.bfloat16),
        ),
        scratch_shapes=[
            pltpu.VMEM((tokens, width), jnp.float32),
            pltpu.VMEM((pairs, width), jnp.float32),
            pltpu.VMEM((tokens, pairs * 128), jnp.float32),
            pltpu.VMEM((2 * pairs * 8, 128), jnp.float32),
        ],
        compiler_params=pltpu.CompilerParams(vmem_limit_bytes=20 * MIB + 512 * pairs * tokens),
        cost_estimate=pl.CostEstimate(
            flops=14 * tokens * width * pairs,
            bytes_accessed=4 * tokens * width,
            transcendentals=2 * tokens * width * pairs,
        ),
        name="score_sums",
    )(ranks, arrived, base, readout)


def direction_kernel(rows_ref, scaled_ref, out_ref):
    out_ref[...] = lax.dot_general(
        rows_ref[0], scaled_ref[...], (((0,), (0,)), ((), ())),
        preferred_element_type=jnp.float32,
    ).astype(jnp.bfloat16)


def make_direction(arrived, scaled, depth):
    cores = arrived.shape[0]
    pairs, width = scaled.shape
    block = 2048
    each = depth // cores // block
    return pl.pallas_call(
        direction_kernel,
        grid=(depth // block,),
        in_specs=[
            pl.BlockSpec((1, pairs, block), lambda i: (i // each, 0, i % each)),
            pl.BlockSpec((pairs, width), lambda i: (0, 0)),
        ],
        out_specs=pl.BlockSpec((block, width), lambda i: (i, 0)),
        out_shape=jax.ShapeDtypeStruct((depth, width), jnp.bfloat16),
        compiler_params=pltpu.CompilerParams(vmem_limit_bytes=20 * MIB),
        cost_estimate=pl.CostEstimate(
            flops=2 * pairs * depth * width, bytes_accessed=2 * depth * width, transcendentals=0
        ),
        name="direction",
    )(arrived, scaled)


def solution(mesh):
    pop, mp = mesh.shape["pop"], mesh.shape["mp"]

    def per_device(prompt_states, weight_codes, block_scales, readout, noise_rows, noise_cols, ranks):
        depth = weight_codes.shape[0]
        own = noise_rows.shape[0]
        parcel = make_parcel(prompt_states, noise_rows, noise_cols, pop * mp, mp)
        arrived = lax.all_to_all(parcel, ("pop", "mp"), split_axis=0, concat_axis=0, tiled=True)
        arrived = arrived.reshape(pop, mp, own, parcel.shape[2]).transpose(1, 0, 2, 3)
        arrived = arrived.reshape(mp, pop * own, parcel.shape[2])

        base = code_base(prompt_states, weight_codes, block_scales.T)

        sums, scaled = score_sums(ranks, arrived, base, readout[None, :], pop * mp)
        everyone = lax.all_to_all(
            sums[:, None, :], ("pop", "mp"), split_axis=0, concat_axis=0, tiled=True
        )
        direction = make_direction(arrived, scaled, depth)
        scores = jnp.sum(everyone, axis=(0, 1)) * (1.0 / math.sqrt(TOK * FF))
        return (direction, scores)

    in_specs = (
        P("parts", None),
        P(None, ("pop", "mp")),
        P(None, ("pop", "mp")),
        P(("pop", "mp")),
        P(("parts", "pop"), None),
        P(("parts", "pop"), None),
        P("parts"),
    )
    out_specs = (P("parts", ("pop", "mp")), P("parts"))
    return jax.shard_map(
        per_device, mesh=mesh, in_specs=in_specs, out_specs=out_specs, check_vma=False
    )
```

```python
import math

import jax
import jax.numpy as jnp
from jax import lax
from jax.experimental import pallas as pl
from jax.experimental.pallas import tpu as pltpu
from jax.sharding import PartitionSpec as P

FF = 16384
BLK = 128
TOK = 512
SIGMA_NOISE = 0.5
STEP_SIZE = 1.0
MIB = 1 << 20


def split3(value):
    hi = value.astype(jnp.bfloat16)
    rest = value - hi.astype(jnp.float32)
    mid = rest.astype(jnp.bfloat16)
    low = (rest - mid.astype(jnp.float32)).astype(jnp.bfloat16)
    return hi, mid, low


def parcel_kernel(
    states_hbm, rows_hbm, cols_hbm, out_ref, states_ref, rows_ref, cols_ref, proj_ref,
    sems, row_sem, col_sem,
):
    members, own, total = out_ref.shape
    share, depth = states_ref.shape
    width = cols_ref.shape[1] // members
    depth_share = total - width - 3 * share
    core = lax.axis_index("mp")
    first_token = pl.multiple_of(core * share, share)
    first_row = pl.multiple_of(core * depth_share, depth_share)
    count = sems.shape[0]
    chunk = depth // count
    ahead = 2

    def state_copy(k):
        span = pl.ds(pl.multiple_of(k * chunk, chunk), chunk)
        return pltpu.make_async_copy(
            states_hbm.at[pl.ds(first_token, share), span], states_ref.at[:, span], sems.at[k]
        )

    row_copy = pltpu.make_async_copy(rows_hbm, rows_ref, row_sem)
    col_copy = pltpu.make_async_copy(cols_hbm, cols_ref, col_sem)
    row_copy.start()
    col_copy.start()
    for k in range(ahead):
        state_copy(k).start()
    row_copy.wait()
    col_copy.wait()
    rows = rows_ref[:, pl.ds(first_row, depth_share)]
    for dest in range(members):
        out_ref[dest, :, :depth_share] = rows
        out_ref[dest, :, depth_share : depth_share + width] = cols_ref[
            :, dest * width : (dest + 1) * width
        ]
    proj_ref[...] = jnp.zeros_like(proj_ref)

    @pl.loop(0, count)
    def _(k):
        state_copy(k).wait()

        @pl.when(k + ahead < count)
        def _():
            state_copy(k + ahead).start()

        span = pl.ds(pl.multiple_of(k * chunk, chunk), chunk)
        proj_ref[...] += lax.dot_general(
            states_ref[:, span], rows_ref[:, span], (((1,), (1,)), ((), ())),
            preferred_element_type=jnp.float32,
        )

    proj = proj_ref[...].T * (1.0 / math.sqrt(depth))
    parts = jnp.concatenate(split3(proj), axis=1)
    for dest in range(members):
        out_ref[dest, :, depth_share + width :] = parts


def make_parcel(states, rows, cols, members, cores):
    own, depth = rows.shape
    tokens = states.shape[0]
    width = cols.shape[1] // members
    share = tokens // cores
    count = 4
    return pl.pallas_call(
        parcel_kernel,
        in_specs=[pl.BlockSpec(memory_space=pltpu.HBM)] * 3,
        out_specs=pl.BlockSpec(memory_space=pltpu.VMEM),
        out_shape=jax.ShapeDtypeStruct(
            (members, own, depth // cores + width + 3 * share), jnp.bfloat16
        ),
        scratch_shapes=[
            pltpu.VMEM((share, depth), jnp.bfloat16),
            pltpu.VMEM(rows.shape, jnp.bfloat16),
            pltpu.VMEM(cols.shape, jnp.bfloat16),
            pltpu.VMEM((share, own), jnp.float32),
            pltpu.SemaphoreType.DMA((count,)),
            pltpu.SemaphoreType.DMA,
            pltpu.SemaphoreType.DMA,
        ],
        compiler_params=pltpu.CompilerParams(vmem_limit_bytes=60 * MIB),
        cost_estimate=pl.CostEstimate(
            flops=5 * 10**9, bytes_accessed=2 * share * depth, transcendentals=0
        ),
        name="parcel",
    )(states, rows, cols)


def code_base_kernel(
    scales_hbm, states_hbm, codes_hbm, out_ref, states_ref, codes_ref, scales_ref,
    scale_sem, state_sems, code_sems,
):
    depth, width = codes_ref.shape
    cuts = chunk_cuts(depth)
    count = len(cuts) - 1
    ahead = 3

    def copies(k):
        span = pl.ds(cuts[k], cuts[k + 1] - cuts[k])
        return (
            pltpu.make_async_copy(states_hbm.at[:, span], states_ref.at[:, span], state_sems.at[k]),
            pltpu.make_async_copy(codes_hbm.at[span, :], codes_ref.at[span, :], code_sems.at[k]),
        )

    scale_copy = pltpu.make_async_copy(scales_hbm, scales_ref, scale_sem)
    scale_copy.start()
    for k in range(min(ahead, count)):
        for copy in copies(k):
            copy.start()
    scale_copy.wait()
    for k in range(count):
        if k + ahead < count:
            for copy in copies(k + ahead):
                copy.start()
        for copy in copies(k):
            copy.wait()
        rows = []
        for i in range(cuts[k], cuts[k + 1], BLK):
            cols = []
            for c in range(0, width, BLK):
                block = codes_ref[i : i + BLK, c : c + BLK].astype(jnp.float32)
                cols.append((block * scales_ref[c // BLK, i // BLK]).astype(jnp.bfloat16))
            rows.append(jnp.concatenate(cols, axis=1) if len(cols) > 1 else cols[0])
        weights = jnp.concatenate(rows, axis=0)
        part = jnp.dot(
            states_ref[:, cuts[k] : cuts[k + 1]], weights, preferred_element_type=jnp.float32
        )
        if k == 0:
            out_ref[...] = part
        else:
            out_ref[...] += part


def chunk_cuts(depth):
    unit = depth // 32
    cuts = [0]
    for size in (1, 3) + (4,) * 7:
        cuts.append(cuts[-1] + size * unit)
    return cuts


def code_base(states, codes, scales_t):
    tokens, depth = states.shape
    width = codes.shape[1]
    count = len(chunk_cuts(depth)) - 1
    vmem = pl.BlockSpec(memory_space=pltpu.VMEM)
    away = pl.BlockSpec(memory_space=pltpu.HBM)
    return pl.pallas_call(
        code_base_kernel,
        in_specs=[away, away, away],
        out_specs=vmem,
        out_shape=jax.ShapeDtypeStruct((tokens, width), jnp.float32),
        scratch_shapes=[
            pltpu.VMEM((tokens, depth), jnp.bfloat16),
            pltpu.VMEM((depth, width), jnp.bfloat16),
            pltpu.SMEM(scales_t.shape, jnp.float32),
            pltpu.SemaphoreType.DMA,
            pltpu.SemaphoreType.DMA((count,)),
            pltpu.SemaphoreType.DMA((count,)),
        ],
        compiler_params=pltpu.CompilerParams(vmem_limit_bytes=48 * MIB),
        cost_estimate=pl.CostEstimate(
            flops=2 * tokens * depth * width,
            bytes_accessed=2 * depth * (tokens + width),
            transcendentals=0,
        ),
        name="code_base",
    )(scales_t, states, codes)


def score_kernel(
    ranks_ref, arrived_ref, base_ref, readout_ref, out_ref, scaled_ref,
    half_ref, cols_ref, factor_ref, terms_ref,
):
    tokens, width = base_ref.shape
    cores, pairs, total = arrived_ref.shape
    share = tokens // cores
    depth_share = total - width - 3 * share
    cols_ref[...] = arrived_ref[0, :, depth_share : depth_share + width].astype(jnp.float32)
    parts = []
    for i in range(3):
        start = depth_share + width + i * share
        parts.append(
            jnp.concatenate(
                [arrived_ref[k, :, start : start + share] for k in range(cores)], axis=1
            )
        )
    split = jnp.concatenate(parts, axis=0)
    over_pairs = (((0,), (0,)), ((), ()))
    which = lax.broadcasted_iota(jnp.int32, (pairs, 128), 0)
    gap = jnp.zeros((pairs, 128), jnp.float32)
    for q in range(pairs):
        mine = (ranks_ref[q] - ranks_ref[q + pairs]).astype(jnp.float32)
        gap = jnp.where(which == q, mine, gap)
    pair_weight = gap / (2 * pairs - 1)
    scaled = (
        jnp.concatenate([pair_weight] * (width // 128), axis=1)
        * cols_ref[...] * (1.0 / math.sqrt(pairs))
    ).astype(jnp.bfloat16)
    scaled_ref[...] = scaled
    step = lax.dot_general(
        split, jnp.concatenate([scaled, scaled, scaled], axis=0), over_pairs,
        preferred_element_type=jnp.float32,
    )
    half_ref[...] = (base_ref[...] + STEP_SIZE * step) * 0.5
    group = min(pairs, 16)
    for first in range(0, pairs, group):
        at = lax.broadcasted_iota(jnp.int32, (3 * pairs, group * 128), 0)
        lane = lax.broadcasted_iota(jnp.int32, (3 * pairs, group * 128), 1)
        goal = first + lane // 128
        hit = (at == goal) | (at == goal + pairs) | (at == goal + 2 * pairs)
        pick = jnp.where(hit, 0.5 * SIGMA_NOISE, 0.0).astype(jnp.bfloat16)
        factor_ref[:, first * 128 : (first + group) * 128] = lax.dot_general(
            split, pick, over_pairs, preferred_element_type=jnp.float32
        )

    tile = min(512, width)
    zero = jnp.zeros((8, tile), jnp.float32)

    def eight(i):
        return pl.ds(pl.multiple_of(i * 8, 8), 8)

    def fold(value):
        lanes = value[:, 0:128]
        for j in range(1, tile // 128):
            lanes = lanes + value[:, j * 128 : (j + 1) * 128]
        return lanes

    for start in range(0, width, tile):
        span = slice(start, start + tile)
        readout = jnp.broadcast_to(readout_ref[:, span], (8, tile))

        def rest_step(i, acc):
            u = half_ref[eight(i), span]
            return acc + u * jnp.tanh(u)

        rest = lax.fori_loop(0, tokens // 8, rest_step, zero, unroll=16)

        def one_pair(p, carry):
            col = jnp.broadcast_to(cols_ref[pl.ds(p, 1), span], (8, tile))
            lanes = pl.ds(pl.multiple_of(p * 128, 128), 128)

            def step(i, acc):
                plus, minus, total = acc
                factor = factor_ref[eight(i), lanes]
                u = half_ref[eight(i), span]
                shift = jnp.concatenate([factor] * (tile // 128), axis=1) * col
                up = u + shift
                um = u - shift
                return plus + up * jnp.tanh(up), minus + um * jnp.tanh(um), total + factor

            plus, minus, total = lax.fori_loop(
                0, tokens // 8, step, (zero, zero, jnp.zeros((8, 128), jnp.float32)),
                unroll=32,
            )
            linear = col * jnp.concatenate([total] * (tile // 128), axis=1)
            plus = fold((plus - rest + linear) * readout)
            minus = fold((minus - rest - linear) * readout)
            if start > 0:
                plus += terms_ref[eight(p), :]
                minus += terms_ref[eight(p + pairs), :]
            terms_ref[eight(p), :] = plus
            terms_ref[eight(p + pairs), :] = minus
            return carry

        lax.fori_loop(0, pairs, one_pair, 0)
    sums = jnp.sum(terms_ref[...].reshape(2 * pairs, 8, 128), axis=1)
    sums = jnp.sum(sums.T, axis=0, keepdims=True)
    out_ref[...] = jnp.broadcast_to(sums, out_ref.shape)


def score_sums(ranks, arrived, base, readout, copies):
    tokens, width = base.shape
    pairs = arrived.shape[1]
    vmem = pl.BlockSpec(memory_space=pltpu.VMEM)
    return pl.pallas_call(
        score_kernel,
        in_specs=[pl.BlockSpec(memory_space=pltpu.SMEM), vmem, vmem, vmem],
        out_specs=(vmem, vmem),
        out_shape=(
            jax.ShapeDtypeStruct((copies, 2 * pairs), jnp.float32),
            jax.ShapeDtypeStruct((pairs, width), jnp.bfloat16),
        ),
        scratch_shapes=[
            pltpu.VMEM((tokens, width), jnp.float32),
            pltpu.VMEM((pairs, width), jnp.float32),
            pltpu.VMEM((tokens, pairs * 128), jnp.float32),
            pltpu.VMEM((2 * pairs * 8, 128), jnp.float32),
        ],
        compiler_params=pltpu.CompilerParams(vmem_limit_bytes=20 * MIB + 512 * pairs * tokens),
        cost_estimate=pl.CostEstimate(
            flops=14 * tokens * width * pairs,
            bytes_accessed=4 * tokens * width,
            transcendentals=2 * tokens * width * pairs,
        ),
        name="score_sums",
    )(ranks, arrived, base, readout)


def direction_kernel(arrived_ref, scaled_ref, out_hbm, block_ref, sems):
    slots, block, _ = block_ref.shape
    depth = out_hbm.shape[0]
    cores = arrived_ref.shape[0]
    scaled = scaled_ref[...]

    def copy(i):
        rows = pl.ds(i * block, block)
        return pltpu.make_async_copy(block_ref.at[i % slots], out_hbm.at[rows, :], sems.at[i % slots])

    count = depth // block
    each = count // cores
    for i in range(count):
        if i >= slots:
            copy(i - slots).wait()
        start = i % each * block
        block_ref[i % slots] = lax.dot_general(
            arrived_ref[i // each, :, start : start + block], scaled, (((0,), (0,)), ((), ())),
            preferred_element_type=jnp.float32,
        ).astype(jnp.bfloat16)
        copy(i).start()
    for i in range(count - slots, count):
        copy(i).wait()


def make_direction(arrived, scaled, depth):
    pairs, width = scaled.shape
    block, slots = 1024, 4
    vmem = pl.BlockSpec(memory_space=pltpu.VMEM)
    return pl.pallas_call(
        direction_kernel,
        in_specs=[vmem, vmem],
        out_specs=pl.BlockSpec(memory_space=pltpu.HBM),
        out_shape=jax.ShapeDtypeStruct((depth, width), jnp.bfloat16),
        scratch_shapes=[
            pltpu.VMEM((slots, block, width), jnp.bfloat16),
            pltpu.SemaphoreType.DMA((slots,)),
        ],
        compiler_params=pltpu.CompilerParams(vmem_limit_bytes=32 * MIB),
        cost_estimate=pl.CostEstimate(
            flops=2 * pairs * depth * width, bytes_accessed=2 * depth * width, transcendentals=0
        ),
        name="direction",
    )(arrived, scaled)


def solution(mesh):
    pop, mp = mesh.shape["pop"], mesh.shape["mp"]

    def per_device(prompt_states, weight_codes, block_scales, readout, noise_rows, noise_cols, ranks):
        depth = weight_codes.shape[0]
        own = noise_rows.shape[0]
        parcel = make_parcel(prompt_states, noise_rows, noise_cols, pop * mp, mp)
        arrived = lax.all_to_all(parcel, ("pop", "mp"), split_axis=0, concat_axis=0, tiled=True)
        arrived = arrived.reshape(pop, mp, own, parcel.shape[2]).transpose(1, 0, 2, 3)
        arrived = arrived.reshape(mp, pop * own, parcel.shape[2])

        base = code_base(prompt_states, weight_codes, block_scales.T)

        sums, scaled = score_sums(ranks, arrived, base, readout[None, :], pop * mp)
        everyone = lax.all_to_all(
            sums[:, None, :], ("pop", "mp"), split_axis=0, concat_axis=0, tiled=True
        )
        direction = make_direction(arrived, scaled, depth)
        scores = jnp.sum(everyone, axis=(0, 1)) * (1.0 / math.sqrt(TOK * FF))
        return (direction, scores)

    in_specs = (
        P("parts", None),
        P(None, ("pop", "mp")),
        P(None, ("pop", "mp")),
        P(("pop", "mp")),
        P(("parts", "pop"), None),
        P(("parts", "pop"), None),
        P("parts"),
    )
    out_specs = (P("parts", ("pop", "mp")), P("parts"))
    return jax.shard_map(
        per_device, mesh=mesh, in_specs=in_specs, out_specs=out_specs, check_vma=False
    )
```

```python
import math

import jax
import jax.numpy as jnp
from jax import lax
from jax.experimental import pallas as pl
from jax.experimental.pallas import tpu as pltpu
from jax.sharding import PartitionSpec as P

FF = 16384
BLK = 128
TOK = 512
SIGMA_NOISE = 0.5
STEP_SIZE = 1.0
MIB = 1 << 20


def split3(value):
    hi = value.astype(jnp.bfloat16)
    rest = value - hi.astype(jnp.float32)
    mid = rest.astype(jnp.bfloat16)
    low = (rest - mid.astype(jnp.float32)).astype(jnp.bfloat16)
    return hi, mid, low


def col_share(width, cores):
    return width // cores if width % (cores * 128) == 0 else width


def parcel_kernel(
    states_hbm, rows_hbm, cols_hbm, out_ref, states_ref, rows_ref, cols_ref, proj_ref,
    sems, row_sem, col_sem,
):
    members, own, total = out_ref.shape
    share, depth = states_ref.shape
    width = cols_ref.shape[1] // members
    depth_share = depth // (states_hbm.shape[0] // share)
    width_share = total - depth_share - 3 * share
    core = lax.axis_index("mp")
    first_col = core * width_share if width_share < width else 0
    first_token = pl.multiple_of(core * share, share)
    first_row = pl.multiple_of(core * depth_share, depth_share)
    count = sems.shape[0]
    chunk = depth // count
    ahead = 2

    def state_copy(k):
        span = pl.ds(pl.multiple_of(k * chunk, chunk), chunk)
        return pltpu.make_async_copy(
            states_hbm.at[pl.ds(first_token, share), span], states_ref.at[:, span], sems.at[k]
        )

    row_copy = pltpu.make_async_copy(rows_hbm, rows_ref, row_sem)
    col_copy = pltpu.make_async_copy(cols_hbm, cols_ref, col_sem)
    row_copy.start()
    col_copy.start()
    for k in range(ahead):
        state_copy(k).start()
    row_copy.wait()
    col_copy.wait()
    rows = rows_ref[:, pl.ds(first_row, depth_share)]
    for dest in range(members):
        out_ref[dest, :, :depth_share] = rows
        start = pl.multiple_of(dest * width + first_col, width_share)
        out_ref[dest, :, depth_share : depth_share + width_share] = cols_ref[
            :, pl.ds(start, width_share)
        ]
    proj_ref[...] = jnp.zeros_like(proj_ref)

    @pl.loop(0, count)
    def _(k):
        state_copy(k).wait()

        @pl.when(k + ahead < count)
        def _():
            state_copy(k + ahead).start()

        span = pl.ds(pl.multiple_of(k * chunk, chunk), chunk)
        proj_ref[...] += lax.dot_general(
            states_ref[:, span], rows_ref[:, span], (((1,), (1,)), ((), ())),
            preferred_element_type=jnp.float32,
        )

    proj = proj_ref[...].T * (1.0 / math.sqrt(depth))
    parts = jnp.concatenate(split3(proj), axis=1)
    for dest in range(members):
        out_ref[dest, :, depth_share + width_share :] = parts


def make_parcel(states, rows, cols, members, cores):
    own, depth = rows.shape
    tokens = states.shape[0]
    width = cols.shape[1] // members
    share = tokens // cores
    count = 2
    return pl.pallas_call(
        parcel_kernel,
        in_specs=[pl.BlockSpec(memory_space=pltpu.HBM)] * 3,
        out_specs=pl.BlockSpec(memory_space=pltpu.VMEM),
        out_shape=jax.ShapeDtypeStruct(
            (members, own, depth // cores + col_share(width, cores) + 3 * share), jnp.bfloat16
        ),
        scratch_shapes=[
            pltpu.VMEM((share, depth), jnp.bfloat16),
            pltpu.VMEM(rows.shape, jnp.bfloat16),
            pltpu.VMEM(cols.shape, jnp.bfloat16),
            pltpu.VMEM((share, own), jnp.float32),
            pltpu.SemaphoreType.DMA((count,)),
            pltpu.SemaphoreType.DMA,
            pltpu.SemaphoreType.DMA,
        ],
        compiler_params=pltpu.CompilerParams(vmem_limit_bytes=60 * MIB),
        cost_estimate=pl.CostEstimate(
            flops=5 * 10**9, bytes_accessed=2 * share * depth, transcendentals=0
        ),
        name="parcel",
    )(states, rows, cols)


def code_base_kernel(
    scales_hbm, states_hbm, codes_hbm, out_ref, states_ref, codes_ref, scales_ref,
    scale_sem, state_sems, code_sems,
):
    depth, width = codes_ref.shape
    cuts = chunk_cuts(depth)
    count = len(cuts) - 1
    ahead = 3

    def copies(k):
        span = pl.ds(cuts[k], cuts[k + 1] - cuts[k])
        return (
            pltpu.make_async_copy(states_hbm.at[:, span], states_ref.at[:, span], state_sems.at[k]),
            pltpu.make_async_copy(codes_hbm.at[span, :], codes_ref.at[span, :], code_sems.at[k]),
        )

    scale_copy = pltpu.make_async_copy(scales_hbm, scales_ref, scale_sem)
    scale_copy.start()
    for k in range(min(ahead, count)):
        for copy in copies(k):
            copy.start()
    scale_copy.wait()
    for k in range(count):
        if k + ahead < count:
            for copy in copies(k + ahead):
                copy.start()
        for copy in copies(k):
            copy.wait()
        rows = []
        for i in range(cuts[k], cuts[k + 1], BLK):
            cols = []
            for c in range(0, width, BLK):
                block = codes_ref[i : i + BLK, c : c + BLK].astype(jnp.float32)
                cols.append((block * scales_ref[c // BLK, i // BLK]).astype(jnp.bfloat16))
            rows.append(jnp.concatenate(cols, axis=1) if len(cols) > 1 else cols[0])
        weights = jnp.concatenate(rows, axis=0)
        part = jnp.dot(
            states_ref[:, cuts[k] : cuts[k + 1]], weights, preferred_element_type=jnp.float32
        )
        if k == 0:
            out_ref[...] = part
        else:
            out_ref[...] += part


def chunk_cuts(depth):
    unit = depth // 32
    cuts = [0]
    for size in (1, 3) + (4,) * 7:
        cuts.append(cuts[-1] + size * unit)
    return cuts


def code_base(states, codes, scales_t):
    tokens, depth = states.shape
    width = codes.shape[1]
    count = len(chunk_cuts(depth)) - 1
    vmem = pl.BlockSpec(memory_space=pltpu.VMEM)
    away = pl.BlockSpec(memory_space=pltpu.HBM)
    return pl.pallas_call(
        code_base_kernel,
        in_specs=[away, away, away],
        out_specs=vmem,
        out_shape=jax.ShapeDtypeStruct((tokens, width), jnp.float32),
        scratch_shapes=[
            pltpu.VMEM((tokens, depth), jnp.bfloat16),
            pltpu.VMEM((depth, width), jnp.bfloat16),
            pltpu.SMEM(scales_t.shape, jnp.float32),
            pltpu.SemaphoreType.DMA,
            pltpu.SemaphoreType.DMA((count,)),
            pltpu.SemaphoreType.DMA((count,)),
        ],
        compiler_params=pltpu.CompilerParams(vmem_limit_bytes=48 * MIB),
        cost_estimate=pl.CostEstimate(
            flops=2 * tokens * depth * width,
            bytes_accessed=2 * depth * (tokens + width),
            transcendentals=0,
        ),
        name="code_base",
    )(scales_t, states, codes)


def score_kernel(
    ranks_ref, arrived_ref, base_ref, readout_ref, out_ref, scaled_ref,
    half_ref, cols_ref, factor_ref, terms_ref,
):
    tokens, width = base_ref.shape
    cores, pairs, total = arrived_ref.shape
    share = tokens // cores
    width_share = col_share(width, cores)
    depth_share = total - width_share - 3 * share
    for k in range(width // width_share):
        cols_ref[:, k * width_share : (k + 1) * width_share] = arrived_ref[
            k, :, depth_share : depth_share + width_share
        ].astype(jnp.float32)
    parts = []
    for i in range(3):
        start = depth_share + width_share + i * share
        parts.append(
            jnp.concatenate(
                [arrived_ref[k, :, start : start + share] for k in range(cores)], axis=1
            )
        )
    split = jnp.concatenate(parts, axis=0)
    over_pairs = (((0,), (0,)), ((), ()))
    which = lax.broadcasted_iota(jnp.int32, (pairs, 128), 0)
    gap = jnp.zeros((pairs, 128), jnp.float32)
    for q in range(pairs):
        mine = (ranks_ref[q] - ranks_ref[q + pairs]).astype(jnp.float32)
        gap = jnp.where(which == q, mine, gap)
    pair_weight = gap / (2 * pairs - 1)
    scaled = (
        jnp.concatenate([pair_weight] * (width // 128), axis=1)
        * cols_ref[...] * (1.0 / math.sqrt(pairs))
    ).astype(jnp.bfloat16)
    scaled_ref[...] = scaled
    step = lax.dot_general(
        split, jnp.concatenate([scaled, scaled, scaled], axis=0), over_pairs,
        preferred_element_type=jnp.float32,
    )
    half_ref[...] = (base_ref[...] + STEP_SIZE * step) * 0.5
    group = min(pairs, 16)
    for first in range(0, pairs, group):
        at = lax.broadcasted_iota(jnp.int32, (3 * pairs, group * 128), 0)
        lane = lax.broadcasted_iota(jnp.int32, (3 * pairs, group * 128), 1)
        goal = first + lane // 128
        hit = (at == goal) | (at == goal + pairs) | (at == goal + 2 * pairs)
        pick = jnp.where(hit, 0.5 * SIGMA_NOISE, 0.0).astype(jnp.bfloat16)
        factor_ref[:, first * 128 : (first + group) * 128] = lax.dot_general(
            split, pick, over_pairs, preferred_element_type=jnp.float32
        )

    tile = min(512, width)
    zero = jnp.zeros((8, tile), jnp.float32)

    def eight(i):
        return pl.ds(pl.multiple_of(i * 8, 8), 8)

    def fold(value):
        lanes = value[:, 0:128]
        for j in range(1, tile // 128):
            lanes = lanes + value[:, j * 128 : (j + 1) * 128]
        return lanes

    for start in range(0, width, tile):
        span = slice(start, start + tile)
        readout = jnp.broadcast_to(readout_ref[:, span], (8, tile))

        def rest_step(i, acc):
            u = half_ref[eight(i), span]
            return acc + u * jnp.tanh(u)

        rest = lax.fori_loop(0, tokens // 8, rest_step, zero, unroll=64)

        def one_pair(p, carry):
            col = jnp.broadcast_to(cols_ref[pl.ds(p, 1), span], (8, tile))
            lanes = pl.ds(pl.multiple_of(p * 128, 128), 128)

            def step(i, acc):
                plus, minus, total = acc
                factor = factor_ref[eight(i), lanes]
                u = half_ref[eight(i), span]
                shift = jnp.concatenate([factor] * (tile // 128), axis=1) * col
                up = u + shift
                um = u - shift
                return plus + up * jnp.tanh(up), minus + um * jnp.tanh(um), total + factor

            plus, minus, total = lax.fori_loop(
                0, tokens // 8, step, (zero, zero, jnp.zeros((8, 128), jnp.float32)),
                unroll=64,
            )
            linear = col * jnp.concatenate([total] * (tile // 128), axis=1)
            plus = fold((plus - rest + linear) * readout)
            minus = fold((minus - rest - linear) * readout)
            if start > 0:
                plus += terms_ref[eight(p), :]
                minus += terms_ref[eight(p + pairs), :]
            terms_ref[eight(p), :] = plus
            terms_ref[eight(p + pairs), :] = minus
            return carry

        lax.fori_loop(0, pairs, one_pair, 0, unroll=2)
    sums = jnp.sum(terms_ref[...].reshape(2 * pairs, 8, 128), axis=1)
    sums = jnp.sum(sums.T, axis=0, keepdims=True)
    out_ref[...] = jnp.broadcast_to(sums, out_ref.shape)


def score_sums(ranks, arrived, base, readout, copies):
    tokens, width = base.shape
    pairs = arrived.shape[1]
    vmem = pl.BlockSpec(memory_space=pltpu.VMEM)
    return pl.pallas_call(
        score_kernel,
        in_specs=[pl.BlockSpec(memory_space=pltpu.SMEM), vmem, vmem, vmem],
        out_specs=(vmem, vmem),
        out_shape=(
            jax.ShapeDtypeStruct((copies, 2 * pairs), jnp.float32),
            jax.ShapeDtypeStruct((pairs, width), jnp.bfloat16),
        ),
        scratch_shapes=[
            pltpu.VMEM((tokens, width), jnp.float32),
            pltpu.VMEM((pairs, width), jnp.float32),
            pltpu.VMEM((tokens, pairs * 128), jnp.float32),
            pltpu.VMEM((2 * pairs * 8, 128), jnp.float32),
        ],
        compiler_params=pltpu.CompilerParams(vmem_limit_bytes=20 * MIB + 512 * pairs * tokens),
        cost_estimate=pl.CostEstimate(
            flops=14 * tokens * width * pairs,
            bytes_accessed=4 * tokens * width,
            transcendentals=2 * tokens * width * pairs,
        ),
        name="score_sums",
    )(ranks, arrived, base, readout)


def direction_kernel(arrived_ref, scaled_ref, out_hbm, block_ref, sems):
    slots, block, _ = block_ref.shape
    depth = out_hbm.shape[0]
    cores = arrived_ref.shape[0]
    scaled = scaled_ref[...]

    def copy(i):
        rows = pl.ds(i * block, block)
        return pltpu.make_async_copy(block_ref.at[i % slots], out_hbm.at[rows, :], sems.at[i % slots])

    count = depth // block
    each = count // cores
    for i in range(count):
        if i >= slots:
            copy(i - slots).wait()
        start = i % each * block
        block_ref[i % slots] = lax.dot_general(
            arrived_ref[i // each, :, start : start + block], scaled, (((0,), (0,)), ((), ())),
            preferred_element_type=jnp.float32,
        ).astype(jnp.bfloat16)
        copy(i).start()
    for i in range(count - slots, count):
        copy(i).wait()


def make_direction(arrived, scaled, depth):
    pairs, width = scaled.shape
    block, slots = 1024, 4
    vmem = pl.BlockSpec(memory_space=pltpu.VMEM)
    return pl.pallas_call(
        direction_kernel,
        in_specs=[vmem, vmem],
        out_specs=pl.BlockSpec(memory_space=pltpu.HBM),
        out_shape=jax.ShapeDtypeStruct((depth, width), jnp.bfloat16),
        scratch_shapes=[
            pltpu.VMEM((slots, block, width), jnp.bfloat16),
            pltpu.SemaphoreType.DMA((slots,)),
        ],
        compiler_params=pltpu.CompilerParams(vmem_limit_bytes=32 * MIB),
        cost_estimate=pl.CostEstimate(
            flops=2 * pairs * depth * width, bytes_accessed=2 * depth * width, transcendentals=0
        ),
        name="direction",
    )(arrived, scaled)


def solution(mesh):
    pop, mp = mesh.shape["pop"], mesh.shape["mp"]

    def per_device(prompt_states, weight_codes, block_scales, readout, noise_rows, noise_cols, ranks):
        depth = weight_codes.shape[0]
        own = noise_rows.shape[0]
        parcel = make_parcel(prompt_states, noise_rows, noise_cols, pop * mp, mp)
        arrived = lax.all_to_all(parcel, ("pop", "mp"), split_axis=0, concat_axis=0, tiled=True)
        arrived = arrived.reshape(pop, mp, own, parcel.shape[2]).transpose(1, 0, 2, 3)
        arrived = arrived.reshape(mp, pop * own, parcel.shape[2])

        base = code_base(prompt_states, weight_codes, block_scales.T)

        sums, scaled = score_sums(ranks, arrived, base, readout[None, :], pop * mp)
        everyone = lax.all_to_all(
            sums[:, None, :], ("pop", "mp"), split_axis=0, concat_axis=0, tiled=True
        )
        direction = make_direction(arrived, scaled, depth)
        scores = jnp.sum(everyone, axis=(0, 1)) * (1.0 / math.sqrt(TOK * FF))
        return (direction, scores)

    in_specs = (
        P("parts", None),
        P(None, ("pop", "mp")),
        P(None, ("pop", "mp")),
        P(("pop", "mp")),
        P(("parts", "pop"), None),
        P(("parts", "pop"), None),
        P("parts"),
    )
    out_specs = (P("parts", ("pop", "mp")), P("parts"))
    return jax.shard_map(
        per_device, mesh=mesh, in_specs=in_specs, out_specs=out_specs, check_vma=False
    )
```

```python
import math

import jax
import jax.numpy as jnp
from jax import lax
from jax.experimental import pallas as pl
from jax.experimental.pallas import tpu as pltpu
from jax.sharding import PartitionSpec as P

FF = 16384
BLK = 128
TOK = 512
SIGMA_NOISE = 0.5
STEP_SIZE = 1.0
MIB = 1 << 20


def split3(value):
    hi = value.astype(jnp.bfloat16)
    rest = value - hi.astype(jnp.float32)
    mid = rest.astype(jnp.bfloat16)
    low = (rest - mid.astype(jnp.float32)).astype(jnp.bfloat16)
    return hi, mid, low


def col_share(width, cores):
    return width // cores if width % (cores * 128) == 0 else width


def parcel_kernel(
    states_hbm, rows_hbm, cols_hbm, out_ref, states_ref, rows_ref, cols_ref, proj_ref,
    sems, row_sem, col_sem,
):
    members, own, total = out_ref.shape
    share, depth = states_ref.shape
    width = cols_ref.shape[1] // members
    depth_share = depth // (states_hbm.shape[0] // share)
    width_share = total - depth_share - 3 * share
    pop = members * share // states_hbm.shape[0]
    core = lax.axis_index("mp")
    first_col = core * width_share if width_share < width else 0
    first_token = pl.multiple_of(core * share, share)
    first_row = pl.multiple_of(core * depth_share, depth_share)
    count = sems.shape[0]
    chunk = depth // count
    ahead = 2

    def state_copy(k):
        span = pl.ds(pl.multiple_of(k * chunk, chunk), chunk)
        return pltpu.make_async_copy(
            states_hbm.at[pl.ds(first_token, share), span], states_ref.at[:, span], sems.at[k]
        )

    row_copy = pltpu.make_async_copy(rows_hbm, rows_ref, row_sem)
    col_copy = pltpu.make_async_copy(cols_hbm, cols_ref, col_sem)
    row_copy.start()
    col_copy.start()
    for k in range(ahead):
        state_copy(k).start()
    row_copy.wait()
    col_copy.wait()
    rows = rows_ref[:, pl.ds(first_row, depth_share)]
    for dest in range(members):
        out_ref[dest, :, :depth_share] = rows
        there = dest % pop * (members // pop) + dest // pop
        start = pl.multiple_of(there * width + first_col, width_share)
        out_ref[dest, :, depth_share : depth_share + width_share] = cols_ref[
            :, pl.ds(start, width_share)
        ]
    proj_ref[...] = jnp.zeros_like(proj_ref)

    @pl.loop(0, count)
    def _(k):
        state_copy(k).wait()

        @pl.when(k + ahead < count)
        def _():
            state_copy(k + ahead).start()

        span = pl.ds(pl.multiple_of(k * chunk, chunk), chunk)
        proj_ref[...] += lax.dot_general(
            states_ref[:, span], rows_ref[:, span], (((1,), (1,)), ((), ())),
            preferred_element_type=jnp.float32,
        )

    proj = proj_ref[...].T * (1.0 / math.sqrt(depth))
    parts = jnp.concatenate(split3(proj), axis=1)
    for dest in range(members):
        out_ref[dest, :, depth_share + width_share :] = parts


def make_parcel(states, rows, cols, members, cores):
    own, depth = rows.shape
    tokens = states.shape[0]
    width = cols.shape[1] // members
    share = tokens // cores
    count = 2
    return pl.pallas_call(
        parcel_kernel,
        in_specs=[pl.BlockSpec(memory_space=pltpu.HBM)] * 3,
        out_specs=pl.BlockSpec(memory_space=pltpu.VMEM),
        out_shape=jax.ShapeDtypeStruct(
            (members, own, depth // cores + col_share(width, cores) + 3 * share), jnp.bfloat16
        ),
        scratch_shapes=[
            pltpu.VMEM((share, depth), jnp.bfloat16),
            pltpu.VMEM(rows.shape, jnp.bfloat16),
            pltpu.VMEM(cols.shape, jnp.bfloat16),
            pltpu.VMEM((share, own), jnp.float32),
            pltpu.SemaphoreType.DMA((count,)),
            pltpu.SemaphoreType.DMA,
            pltpu.SemaphoreType.DMA,
        ],
        compiler_params=pltpu.CompilerParams(vmem_limit_bytes=60 * MIB),
        cost_estimate=pl.CostEstimate(
            flops=5 * 10**9, bytes_accessed=2 * share * depth, transcendentals=0
        ),
        name="parcel",
    )(states, rows, cols)


def code_base_kernel(
    scales_hbm, states_hbm, codes_hbm, out_ref, states_ref, codes_ref, scales_ref,
    scale_sem, state_sems, code_sems,
):
    depth, width = codes_ref.shape
    cuts = chunk_cuts(depth)
    count = len(cuts) - 1
    ahead = 3

    def copies(k):
        span = pl.ds(cuts[k], cuts[k + 1] - cuts[k])
        return (
            pltpu.make_async_copy(states_hbm.at[:, span], states_ref.at[:, span], state_sems.at[k]),
            pltpu.make_async_copy(codes_hbm.at[span, :], codes_ref.at[span, :], code_sems.at[k]),
        )

    scale_copy = pltpu.make_async_copy(scales_hbm, scales_ref, scale_sem)
    scale_copy.start()
    for k in range(min(ahead, count)):
        for copy in copies(k):
            copy.start()
    scale_copy.wait()
    for k in range(count):
        if k + ahead < count:
            for copy in copies(k + ahead):
                copy.start()
        for copy in copies(k):
            copy.wait()
        rows = []
        for i in range(cuts[k], cuts[k + 1], BLK):
            cols = []
            for c in range(0, width, BLK):
                block = codes_ref[i : i + BLK, c : c + BLK].astype(jnp.float32)
                cols.append((block * scales_ref[c // BLK, i // BLK]).astype(jnp.bfloat16))
            rows.append(jnp.concatenate(cols, axis=1) if len(cols) > 1 else cols[0])
        weights = jnp.concatenate(rows, axis=0)
        part = jnp.dot(
            states_ref[:, cuts[k] : cuts[k + 1]], weights, preferred_element_type=jnp.float32
        )
        if k == 0:
            out_ref[...] = part
        else:
            out_ref[...] += part


def chunk_cuts(depth):
    unit = depth // 32
    cuts = [0]
    for size in (1, 3) + (4,) * 7:
        cuts.append(cuts[-1] + size * unit)
    return cuts


def code_base(states, codes, scales_t):
    tokens, depth = states.shape
    width = codes.shape[1]
    count = len(chunk_cuts(depth)) - 1
    vmem = pl.BlockSpec(memory_space=pltpu.VMEM)
    away = pl.BlockSpec(memory_space=pltpu.HBM)
    return pl.pallas_call(
        code_base_kernel,
        in_specs=[away, away, away],
        out_specs=vmem,
        out_shape=jax.ShapeDtypeStruct((tokens, width), jnp.float32),
        scratch_shapes=[
            pltpu.VMEM((tokens, depth), jnp.bfloat16),
            pltpu.VMEM((depth, width), jnp.bfloat16),
            pltpu.SMEM(scales_t.shape, jnp.float32),
            pltpu.SemaphoreType.DMA,
            pltpu.SemaphoreType.DMA((count,)),
            pltpu.SemaphoreType.DMA((count,)),
        ],
        compiler_params=pltpu.CompilerParams(vmem_limit_bytes=48 * MIB),
        cost_estimate=pl.CostEstimate(
            flops=2 * tokens * depth * width,
            bytes_accessed=2 * depth * (tokens + width),
            transcendentals=0,
        ),
        name="code_base",
    )(scales_t, states, codes)


def score_kernel(
    ranks_ref, arrived_ref, base_ref, readout_ref, out_ref, scaled_ref,
    half_ref, cols_ref, factor_ref, terms_ref,
):
    tokens, width = base_ref.shape
    cores, pairs, total = arrived_ref.shape
    share = tokens // cores
    width_share = col_share(width, cores)
    depth_share = total - width_share - 3 * share
    for k in range(width // width_share):
        cols_ref[:, k * width_share : (k + 1) * width_share] = arrived_ref[
            k, :, depth_share : depth_share + width_share
        ].astype(jnp.float32)
    parts = []
    for i in range(3):
        start = depth_share + width_share + i * share
        parts.append(
            jnp.concatenate(
                [arrived_ref[k, :, start : start + share] for k in range(cores)], axis=1
            )
        )
    split = jnp.concatenate(parts, axis=0)
    over_pairs = (((0,), (0,)), ((), ()))
    which = lax.broadcasted_iota(jnp.int32, (pairs, 128), 0)
    gap = jnp.zeros((pairs, 128), jnp.float32)
    for q in range(pairs):
        mine = (ranks_ref[q] - ranks_ref[q + pairs]).astype(jnp.float32)
        gap = jnp.where(which == q, mine, gap)
    pair_weight = gap / (2 * pairs - 1)
    scaled = (
        jnp.concatenate([pair_weight] * (width // 128), axis=1)
        * cols_ref[...] * (1.0 / math.sqrt(pairs))
    ).astype(jnp.bfloat16)
    scaled_ref[...] = scaled
    step = lax.dot_general(
        split, jnp.concatenate([scaled, scaled, scaled], axis=0), over_pairs,
        preferred_element_type=jnp.float32,
    )
    half_ref[...] = (base_ref[...] + STEP_SIZE * step) * 0.5
    group = min(pairs, 16)
    for first in range(0, pairs, group):
        at = lax.broadcasted_iota(jnp.int32, (3 * pairs, group * 128), 0)
        lane = lax.broadcasted_iota(jnp.int32, (3 * pairs, group * 128), 1)
        goal = first + lane // 128
        hit = (at == goal) | (at == goal + pairs) | (at == goal + 2 * pairs)
        pick = jnp.where(hit, 0.5 * SIGMA_NOISE, 0.0).astype(jnp.bfloat16)
        factor_ref[:, first * 128 : (first + group) * 128] = lax.dot_general(
            split, pick, over_pairs, preferred_element_type=jnp.float32
        )

    tile = min(512, width)
    zero = jnp.zeros((8, tile), jnp.float32)

    def eight(i):
        return pl.ds(pl.multiple_of(i * 8, 8), 8)

    def fold(value):
        lanes = value[:, 0:128]
        for j in range(1, tile // 128):
            lanes = lanes + value[:, j * 128 : (j + 1) * 128]
        return lanes

    for start in range(0, width, tile):
        span = slice(start, start + tile)
        readout = jnp.broadcast_to(readout_ref[:, span], (8, tile))

        def rest_step(i, acc):
            u = half_ref[eight(i), span]
            return acc + u * jnp.tanh(u)

        rest = lax.fori_loop(0, tokens // 8, rest_step, zero, unroll=64)

        def one_pair(p, carry):
            col = jnp.broadcast_to(cols_ref[pl.ds(p, 1), span], (8, tile))
            lanes = pl.ds(pl.multiple_of(p * 128, 128), 128)

            def step(i, acc):
                plus, minus, total = acc
                factor = factor_ref[eight(i), lanes]
                u = half_ref[eight(i), span]
                shift = jnp.concatenate([factor] * (tile // 128), axis=1) * col
                up = u + shift
                um = u - shift
                return plus + up * jnp.tanh(up), minus + um * jnp.tanh(um), total + factor

            plus, minus, total = lax.fori_loop(
                0, tokens // 8, step, (zero, zero, jnp.zeros((8, 128), jnp.float32)),
                unroll=64,
            )
            linear = col * jnp.concatenate([total] * (tile // 128), axis=1)
            plus = fold((plus - rest + linear) * readout)
            minus = fold((minus - rest - linear) * readout)
            if start > 0:
                plus += terms_ref[eight(p), :]
                minus += terms_ref[eight(p + pairs), :]
            terms_ref[eight(p), :] = plus
            terms_ref[eight(p + pairs), :] = minus
            return carry

        lax.fori_loop(0, pairs, one_pair, 0, unroll=2)
    sums = jnp.sum(terms_ref[...].reshape(2 * pairs, 8, 128), axis=1)
    sums = jnp.sum(sums.T, axis=0, keepdims=True)
    out_ref[...] = jnp.broadcast_to(sums, out_ref.shape)


def score_sums(ranks, arrived, base, readout, copies):
    tokens, width = base.shape
    pairs = arrived.shape[1]
    vmem = pl.BlockSpec(memory_space=pltpu.VMEM)
    return pl.pallas_call(
        score_kernel,
        in_specs=[pl.BlockSpec(memory_space=pltpu.SMEM), vmem, vmem, vmem],
        out_specs=(vmem, vmem),
        out_shape=(
            jax.ShapeDtypeStruct((copies, 2 * pairs), jnp.float32),
            jax.ShapeDtypeStruct((pairs, width), jnp.bfloat16),
        ),
        scratch_shapes=[
            pltpu.VMEM((tokens, width), jnp.float32),
            pltpu.VMEM((pairs, width), jnp.float32),
            pltpu.VMEM((tokens, pairs * 128), jnp.float32),
            pltpu.VMEM((2 * pairs * 8, 128), jnp.float32),
        ],
        compiler_params=pltpu.CompilerParams(vmem_limit_bytes=20 * MIB + 512 * pairs * tokens),
        cost_estimate=pl.CostEstimate(
            flops=14 * tokens * width * pairs,
            bytes_accessed=4 * tokens * width,
            transcendentals=2 * tokens * width * pairs,
        ),
        name="score_sums",
    )(ranks, arrived, base, readout)


def direction_kernel(arrived_ref, scaled_ref, out_hbm, block_ref, sems):
    slots, block, _ = block_ref.shape
    depth = out_hbm.shape[0]
    cores = arrived_ref.shape[0]
    scaled = scaled_ref[...]

    def copy(i):
        rows = pl.ds(i * block, block)
        return pltpu.make_async_copy(block_ref.at[i % slots], out_hbm.at[rows, :], sems.at[i % slots])

    count = depth // block
    each = count // cores
    for i in range(count):
        if i >= slots:
            copy(i - slots).wait()
        start = i % each * block
        block_ref[i % slots] = lax.dot_general(
            arrived_ref[i // each, :, start : start + block], scaled, (((0,), (0,)), ((), ())),
            preferred_element_type=jnp.float32,
        ).astype(jnp.bfloat16)
        copy(i).start()
    for i in range(count - slots, count):
        copy(i).wait()


def make_direction(arrived, scaled, depth):
    pairs, width = scaled.shape
    block, slots = 1024, 4
    vmem = pl.BlockSpec(memory_space=pltpu.VMEM)
    return pl.pallas_call(
        direction_kernel,
        in_specs=[vmem, vmem],
        out_specs=pl.BlockSpec(memory_space=pltpu.HBM),
        out_shape=jax.ShapeDtypeStruct((depth, width), jnp.bfloat16),
        scratch_shapes=[
            pltpu.VMEM((slots, block, width), jnp.bfloat16),
            pltpu.SemaphoreType.DMA((slots,)),
        ],
        compiler_params=pltpu.CompilerParams(vmem_limit_bytes=32 * MIB),
        cost_estimate=pl.CostEstimate(
            flops=2 * pairs * depth * width, bytes_accessed=2 * depth * width, transcendentals=0
        ),
        name="direction",
    )(arrived, scaled)


def solution(mesh):
    pop, mp = mesh.shape["pop"], mesh.shape["mp"]

    def per_device(prompt_states, weight_codes, block_scales, readout, noise_rows, noise_cols, ranks):
        depth = weight_codes.shape[0]
        own = noise_rows.shape[0]
        parcel = make_parcel(prompt_states, noise_rows, noise_cols, pop * mp, mp)
        arrived = lax.all_to_all(parcel, ("mp", "pop"), split_axis=0, concat_axis=0, tiled=True)
        arrived = arrived.reshape(mp, pop * own, parcel.shape[2])

        base = code_base(prompt_states, weight_codes, block_scales.T)

        sums, scaled = score_sums(ranks, arrived, base, readout[None, :], pop * mp)
        everyone = lax.all_to_all(
            sums[:, None, :], ("pop", "mp"), split_axis=0, concat_axis=0, tiled=True
        )
        direction = make_direction(arrived, scaled, depth)
        scores = jnp.sum(everyone, axis=(0, 1)) * (1.0 / math.sqrt(TOK * FF))
        return (direction, scores)

    in_specs = (
        P("parts", None),
        P(None, ("pop", "mp")),
        P(None, ("pop", "mp")),
        P(("pop", "mp")),
        P(("parts", "pop"), None),
        P(("parts", "pop"), None),
        P("parts"),
    )
    out_specs = (P("parts", ("pop", "mp")), P("parts"))
    return jax.shard_map(
        per_device, mesh=mesh, in_specs=in_specs, out_specs=out_specs, check_vma=False
    )
```

```python
import math

import jax
import jax.numpy as jnp
from jax import lax
from jax.experimental import pallas as pl
from jax.experimental.pallas import tpu as pltpu
from jax.sharding import PartitionSpec as P

FF = 16384
BLK = 128
TOK = 512
SIGMA_NOISE = 0.5
STEP_SIZE = 1.0
MIB = 1 << 20


def split2(value):
    hi = value.astype(jnp.bfloat16)
    return hi, (value - hi.astype(jnp.float32)).astype(jnp.bfloat16)


def col_share(width, cores):
    return width // cores if width % (cores * 128) == 0 else width


def parcel_kernel(
    states_hbm, rows_hbm, cols_hbm, out_ref, states_ref, rows_ref, cols_ref, proj_ref,
    sems, row_sem, col_sem,
):
    members, own, total = out_ref.shape
    share, depth = states_ref.shape
    width = cols_ref.shape[1] // members
    depth_share = depth // (states_hbm.shape[0] // share)
    width_share = total - depth_share - 2 * share
    pop = members * share // states_hbm.shape[0]
    core = lax.axis_index("mp")
    first_col = core * width_share if width_share < width else 0
    first_token = pl.multiple_of(core * share, share)
    first_row = pl.multiple_of(core * depth_share, depth_share)
    count = sems.shape[0]
    chunk = depth // count
    ahead = 2

    def state_copy(k):
        span = pl.ds(pl.multiple_of(k * chunk, chunk), chunk)
        return pltpu.make_async_copy(
            states_hbm.at[pl.ds(first_token, share), span], states_ref.at[:, span], sems.at[k]
        )

    row_copy = pltpu.make_async_copy(rows_hbm, rows_ref, row_sem)
    col_copy = pltpu.make_async_copy(cols_hbm, cols_ref, col_sem)
    row_copy.start()
    col_copy.start()
    for k in range(ahead):
        state_copy(k).start()
    row_copy.wait()
    col_copy.wait()
    rows = rows_ref[:, pl.ds(first_row, depth_share)]
    for dest in range(members):
        out_ref[dest, :, :depth_share] = rows
        there = dest % pop * (members // pop) + dest // pop
        start = pl.multiple_of(there * width + first_col, width_share)
        out_ref[dest, :, depth_share : depth_share + width_share] = cols_ref[
            :, pl.ds(start, width_share)
        ]
    proj_ref[...] = jnp.zeros_like(proj_ref)

    @pl.loop(0, count)
    def _(k):
        state_copy(k).wait()

        @pl.when(k + ahead < count)
        def _():
            state_copy(k + ahead).start()

        span = pl.ds(pl.multiple_of(k * chunk, chunk), chunk)
        proj_ref[...] += lax.dot_general(
            states_ref[:, span], rows_ref[:, span], (((1,), (1,)), ((), ())),
            preferred_element_type=jnp.float32,
        )

    proj = proj_ref[...].T * (1.0 / math.sqrt(depth))
    parts = jnp.concatenate(split2(proj), axis=1)
    for dest in range(members):
        out_ref[dest, :, depth_share + width_share :] = parts


def make_parcel(states, rows, cols, members, cores):
    own, depth = rows.shape
    tokens = states.shape[0]
    width = cols.shape[1] // members
    share = tokens // cores
    count = 2
    return pl.pallas_call(
        parcel_kernel,
        in_specs=[pl.BlockSpec(memory_space=pltpu.HBM)] * 3,
        out_specs=pl.BlockSpec(memory_space=pltpu.VMEM),
        out_shape=jax.ShapeDtypeStruct(
            (members, own, depth // cores + col_share(width, cores) + 2 * share), jnp.bfloat16
        ),
        scratch_shapes=[
            pltpu.VMEM((share, depth), jnp.bfloat16),
            pltpu.VMEM(rows.shape, jnp.bfloat16),
            pltpu.VMEM(cols.shape, jnp.bfloat16),
            pltpu.VMEM((share, own), jnp.float32),
            pltpu.SemaphoreType.DMA((count,)),
            pltpu.SemaphoreType.DMA,
            pltpu.SemaphoreType.DMA,
        ],
        compiler_params=pltpu.CompilerParams(vmem_limit_bytes=60 * MIB),
        cost_estimate=pl.CostEstimate(
            flops=5 * 10**9, bytes_accessed=2 * share * depth, transcendentals=0
        ),
        name="parcel",
    )(states, rows, cols)


def code_base_kernel(
    scales_hbm, states_hbm, codes_hbm, out_ref, states_ref, codes_ref, scales_ref,
    scale_sem, state_sems, code_sems,
):
    depth, width = codes_ref.shape
    cuts = chunk_cuts(depth)
    count = len(cuts) - 1
    ahead = 3

    def copies(k):
        span = pl.ds(cuts[k], cuts[k + 1] - cuts[k])
        return (
            pltpu.make_async_copy(states_hbm.at[:, span], states_ref.at[:, span], state_sems.at[k]),
            pltpu.make_async_copy(codes_hbm.at[span, :], codes_ref.at[span, :], code_sems.at[k]),
        )

    scale_copy = pltpu.make_async_copy(scales_hbm, scales_ref, scale_sem)
    scale_copy.start()
    for k in range(min(ahead, count)):
        for copy in copies(k):
            copy.start()
    scale_copy.wait()
    for k in range(count):
        if k + ahead < count:
            for copy in copies(k + ahead):
                copy.start()
        for copy in copies(k):
            copy.wait()
        rows = []
        for i in range(cuts[k], cuts[k + 1], BLK):
            cols = []
            for c in range(0, width, BLK):
                block = codes_ref[i : i + BLK, c : c + BLK].astype(jnp.float32)
                cols.append((block * scales_ref[c // BLK, i // BLK]).astype(jnp.bfloat16))
            rows.append(jnp.concatenate(cols, axis=1) if len(cols) > 1 else cols[0])
        weights = jnp.concatenate(rows, axis=0)
        part = jnp.dot(
            states_ref[:, cuts[k] : cuts[k + 1]], weights, preferred_element_type=jnp.float32
        )
        if k == 0:
            out_ref[...] = part
        else:
            out_ref[...] += part


def chunk_cuts(depth):
    unit = depth // 32
    cuts = [0]
    for size in (1, 3) + (4,) * 7:
        cuts.append(cuts[-1] + size * unit)
    return cuts


def code_base(states, codes, scales_t):
    tokens, depth = states.shape
    width = codes.shape[1]
    count = len(chunk_cuts(depth)) - 1
    vmem = pl.BlockSpec(memory_space=pltpu.VMEM)
    away = pl.BlockSpec(memory_space=pltpu.HBM)
    return pl.pallas_call(
        code_base_kernel,
        in_specs=[away, away, away],
        out_specs=vmem,
        out_shape=jax.ShapeDtypeStruct((tokens, width), jnp.float32),
        scratch_shapes=[
            pltpu.VMEM((tokens, depth), jnp.bfloat16),
            pltpu.VMEM((depth, width), jnp.bfloat16),
            pltpu.SMEM(scales_t.shape, jnp.float32),
            pltpu.SemaphoreType.DMA,
            pltpu.SemaphoreType.DMA((count,)),
            pltpu.SemaphoreType.DMA((count,)),
        ],
        compiler_params=pltpu.CompilerParams(vmem_limit_bytes=48 * MIB),
        cost_estimate=pl.CostEstimate(
            flops=2 * tokens * depth * width,
            bytes_accessed=2 * depth * (tokens + width),
            transcendentals=0,
        ),
        name="code_base",
    )(scales_t, states, codes)


def score_kernel(
    ranks_ref, arrived_ref, base_ref, readout_ref, out_ref, scaled_ref,
    half_ref, cols_ref, factor_ref, terms_ref,
):
    tokens, width = base_ref.shape
    cores, pairs, total = arrived_ref.shape
    share = tokens // cores
    width_share = col_share(width, cores)
    depth_share = total - width_share - 2 * share
    for k in range(width // width_share):
        cols_ref[:, k * width_share : (k + 1) * width_share] = arrived_ref[
            k, :, depth_share : depth_share + width_share
        ].astype(jnp.float32)
    parts = []
    for i in range(2):
        start = depth_share + width_share + i * share
        parts.append(
            jnp.concatenate(
                [arrived_ref[k, :, start : start + share] for k in range(cores)], axis=1
            )
        )
    split = jnp.concatenate(parts, axis=0)
    over_pairs = (((0,), (0,)), ((), ()))
    which = lax.broadcasted_iota(jnp.int32, (pairs, 128), 0)
    gap = jnp.zeros((pairs, 128), jnp.float32)
    for q in range(pairs):
        mine = (ranks_ref[q] - ranks_ref[q + pairs]).astype(jnp.float32)
        gap = jnp.where(which == q, mine, gap)
    pair_weight = gap / (2 * pairs - 1)
    scaled = (
        jnp.concatenate([pair_weight] * (width // 128), axis=1)
        * cols_ref[...] * (1.0 / math.sqrt(pairs))
    ).astype(jnp.bfloat16)
    scaled_ref[...] = scaled
    step = lax.dot_general(
        split, jnp.concatenate([scaled, scaled], axis=0), over_pairs,
        preferred_element_type=jnp.float32,
    )
    half_ref[...] = (base_ref[...] + STEP_SIZE * step) * 0.5
    group = min(pairs, 16)
    for first in range(0, pairs, group):
        at = lax.broadcasted_iota(jnp.int32, (2 * pairs, group * 128), 0)
        lane = lax.broadcasted_iota(jnp.int32, (2 * pairs, group * 128), 1)
        goal = first + lane // 128
        hit = (at == goal) | (at == goal + pairs)
        pick = jnp.where(hit, 0.5 * SIGMA_NOISE, 0.0).astype(jnp.bfloat16)
        factor_ref[:, first * 128 : (first + group) * 128] = lax.dot_general(
            split, pick, over_pairs, preferred_element_type=jnp.float32
        )

    tile = min(512, width)
    zero = jnp.zeros((8, tile), jnp.float32)

    def eight(i):
        return pl.ds(pl.multiple_of(i * 8, 8), 8)

    def fold(value):
        lanes = value[:, 0:128]
        for j in range(1, tile // 128):
            lanes = lanes + value[:, j * 128 : (j + 1) * 128]
        return lanes

    for start in range(0, width, tile):
        span = slice(start, start + tile)
        readout = jnp.broadcast_to(readout_ref[:, span], (8, tile))

        def rest_step(i, acc):
            u = half_ref[eight(i), span]
            return acc + u * jnp.tanh(u)

        rest = lax.fori_loop(0, tokens // 8, rest_step, zero, unroll=64)

        def one_pair(p, carry):
            col = jnp.broadcast_to(cols_ref[pl.ds(p, 1), span], (8, tile))
            lanes = pl.ds(pl.multiple_of(p * 128, 128), 128)

            def step(i, acc):
                plus, minus, total = acc
                factor = factor_ref[eight(i), lanes]
                u = half_ref[eight(i), span]
                shift = jnp.concatenate([factor] * (tile // 128), axis=1) * col
                up = u + shift
                um = u - shift
                return plus + up * jnp.tanh(up), minus + um * jnp.tanh(um), total + factor

            plus, minus, total = lax.fori_loop(
                0, tokens // 8, step, (zero, zero, jnp.zeros((8, 128), jnp.float32)),
                unroll=64,
            )
            linear = col * jnp.concatenate([total] * (tile // 128), axis=1)
            plus = fold((plus - rest + linear) * readout)
            minus = fold((minus - rest - linear) * readout)
            if start > 0:
                plus += terms_ref[eight(p), :]
                minus += terms_ref[eight(p + pairs), :]
            terms_ref[eight(p), :] = plus
            terms_ref[eight(p + pairs), :] = minus
            return carry

        lax.fori_loop(0, pairs, one_pair, 0, unroll=2)
    sums = jnp.sum(terms_ref[...].reshape(2 * pairs, 8, 128), axis=1)
    sums = jnp.sum(sums.T, axis=0, keepdims=True)
    out_ref[...] = jnp.broadcast_to(sums, out_ref.shape)


def score_sums(ranks, arrived, base, readout, copies):
    tokens, width = base.shape
    pairs = arrived.shape[1]
    vmem = pl.BlockSpec(memory_space=pltpu.VMEM)
    return pl.pallas_call(
        score_kernel,
        in_specs=[pl.BlockSpec(memory_space=pltpu.SMEM), vmem, vmem, vmem],
        out_specs=(vmem, vmem),
        out_shape=(
            jax.ShapeDtypeStruct((copies, 2 * pairs), jnp.float32),
            jax.ShapeDtypeStruct((pairs, width), jnp.bfloat16),
        ),
        scratch_shapes=[
            pltpu.VMEM((tokens, width), jnp.float32),
            pltpu.VMEM((pairs, width), jnp.float32),
            pltpu.VMEM((tokens, pairs * 128), jnp.float32),
            pltpu.VMEM((2 * pairs * 8, 128), jnp.float32),
        ],
        compiler_params=pltpu.CompilerParams(vmem_limit_bytes=20 * MIB + 512 * pairs * tokens),
        cost_estimate=pl.CostEstimate(
            flops=14 * tokens * width * pairs,
            bytes_accessed=4 * tokens * width,
            transcendentals=2 * tokens * width * pairs,
        ),
        name="score_sums",
    )(ranks, arrived, base, readout)


def direction_kernel(arrived_ref, scaled_ref, out_hbm, block_ref, sems):
    slots, block, _ = block_ref.shape
    depth = out_hbm.shape[0]
    cores = arrived_ref.shape[0]
    scaled = scaled_ref[...]

    def copy(i):
        rows = pl.ds(i * block, block)
        return pltpu.make_async_copy(block_ref.at[i % slots], out_hbm.at[rows, :], sems.at[i % slots])

    count = depth // block
    each = count // cores
    for i in range(count):
        if i >= slots:
            copy(i - slots).wait()
        start = i % each * block
        block_ref[i % slots] = lax.dot_general(
            arrived_ref[i // each, :, start : start + block], scaled, (((0,), (0,)), ((), ())),
            preferred_element_type=jnp.float32,
        ).astype(jnp.bfloat16)
        copy(i).start()
    for i in range(count - slots, count):
        copy(i).wait()


def make_direction(arrived, scaled, depth):
    pairs, width = scaled.shape
    block, slots = 1024, 4
    vmem = pl.BlockSpec(memory_space=pltpu.VMEM)
    return pl.pallas_call(
        direction_kernel,
        in_specs=[vmem, vmem],
        out_specs=pl.BlockSpec(memory_space=pltpu.HBM),
        out_shape=jax.ShapeDtypeStruct((depth, width), jnp.bfloat16),
        scratch_shapes=[
            pltpu.VMEM((slots, block, width), jnp.bfloat16),
            pltpu.SemaphoreType.DMA((slots,)),
        ],
        compiler_params=pltpu.CompilerParams(vmem_limit_bytes=32 * MIB),
        cost_estimate=pl.CostEstimate(
            flops=2 * pairs * depth * width, bytes_accessed=2 * depth * width, transcendentals=0
        ),
        name="direction",
    )(arrived, scaled)


def solution(mesh):
    pop, mp = mesh.shape["pop"], mesh.shape["mp"]

    def per_device(prompt_states, weight_codes, block_scales, readout, noise_rows, noise_cols, ranks):
        depth = weight_codes.shape[0]
        own = noise_rows.shape[0]
        parcel = make_parcel(prompt_states, noise_rows, noise_cols, pop * mp, mp)
        arrived = lax.all_to_all(parcel, ("mp", "pop"), split_axis=0, concat_axis=0, tiled=True)
        arrived = arrived.reshape(mp, pop * own, parcel.shape[2])

        base = code_base(prompt_states, weight_codes, block_scales.T)

        sums, scaled = score_sums(ranks, arrived, base, readout[None, :], pop * mp)
        everyone = lax.all_to_all(
            sums[:, None, :], ("pop", "mp"), split_axis=0, concat_axis=0, tiled=True
        )
        direction = make_direction(arrived, scaled, depth)
        scores = jnp.sum(everyone, axis=(0, 1)) * (1.0 / math.sqrt(TOK * FF))
        return (direction, scores)

    in_specs = (
        P("parts", None),
        P(None, ("pop", "mp")),
        P(None, ("pop", "mp")),
        P(("pop", "mp")),
        P(("parts", "pop"), None),
        P(("parts", "pop"), None),
        P("parts"),
    )
    out_specs = (P("parts", ("pop", "mp")), P("parts"))
    return jax.shard_map(
        per_device, mesh=mesh, in_specs=in_specs, out_specs=out_specs, check_vma=False
    )
```

```python
import math

import jax
import jax.numpy as jnp
from jax import lax
from jax.experimental import pallas as pl
from jax.experimental.pallas import tpu as pltpu
from jax.sharding import PartitionSpec as P

FF = 16384
BLK = 128
TOK = 512
SIGMA_NOISE = 0.5
STEP_SIZE = 1.0
MIB = 1 << 20


def split3(value):
    hi = value.astype(jnp.bfloat16)
    rest = value - hi.astype(jnp.float32)
    mid = rest.astype(jnp.bfloat16)
    low = (rest - mid.astype(jnp.float32)).astype(jnp.bfloat16)
    return hi, mid, low


def col_share(width, cores):
    return width // cores if width % (cores * 128) == 0 else width


def parcel_kernel(
    states_hbm, rows_hbm, cols_hbm, out_ref, states_ref, rows_ref, cols_ref, proj_ref,
    sems, row_sem, col_sem,
):
    members, own, total = out_ref.shape
    share, depth = states_ref.shape
    width = cols_ref.shape[1] // members
    depth_share = depth // (states_hbm.shape[0] // share)
    width_share = total - depth_share - 3 * share
    pop = members * share // states_hbm.shape[0]
    core = lax.axis_index("mp")
    first_col = core * width_share if width_share < width else 0
    first_token = pl.multiple_of(core * share, share)
    first_row = pl.multiple_of(core * depth_share, depth_share)
    count = sems.shape[0]
    chunk = depth // count
    ahead = 2

    def state_copy(k):
        span = pl.ds(pl.multiple_of(k * chunk, chunk), chunk)
        return pltpu.make_async_copy(
            states_hbm.at[pl.ds(first_token, share), span], states_ref.at[:, span], sems.at[k]
        )

    row_copy = pltpu.make_async_copy(rows_hbm, rows_ref, row_sem)
    col_copy = pltpu.make_async_copy(cols_hbm, cols_ref, col_sem)
    row_copy.start()
    col_copy.start()
    for k in range(ahead):
        state_copy(k).start()
    row_copy.wait()
    col_copy.wait()
    rows = rows_ref[:, pl.ds(first_row, depth_share)]
    for dest in range(members):
        out_ref[dest, :, :depth_share] = rows
        there = dest % pop * (members // pop) + dest // pop
        start = pl.multiple_of(there * width + first_col, width_share)
        out_ref[dest, :, depth_share : depth_share + width_share] = cols_ref[
            :, pl.ds(start, width_share)
        ]
    proj_ref[...] = jnp.zeros_like(proj_ref)

    @pl.loop(0, count)
    def _(k):
        state_copy(k).wait()

        @pl.when(k + ahead < count)
        def _():
            state_copy(k + ahead).start()

        span = pl.ds(pl.multiple_of(k * chunk, chunk), chunk)
        proj_ref[...] += lax.dot_general(
            states_ref[:, span], rows_ref[:, span], (((1,), (1,)), ((), ())),
            preferred_element_type=jnp.float32,
        )

    proj = proj_ref[...].T * (1.0 / math.sqrt(depth))
    parts = jnp.concatenate(split3(proj), axis=1)
    for dest in range(members):
        out_ref[dest, :, depth_share + width_share :] = parts


def make_parcel(states, rows, cols, members, cores):
    own, depth = rows.shape
    tokens = states.shape[0]
    width = cols.shape[1] // members
    share = tokens // cores
    count = 2
    return pl.pallas_call(
        parcel_kernel,
        in_specs=[pl.BlockSpec(memory_space=pltpu.HBM)] * 3,
        out_specs=pl.BlockSpec(memory_space=pltpu.VMEM),
        out_shape=jax.ShapeDtypeStruct(
            (members, own, depth // cores + col_share(width, cores) + 3 * share), jnp.bfloat16
        ),
        scratch_shapes=[
            pltpu.VMEM((share, depth), jnp.bfloat16),
            pltpu.VMEM(rows.shape, jnp.bfloat16),
            pltpu.VMEM(cols.shape, jnp.bfloat16),
            pltpu.VMEM((share, own), jnp.float32),
            pltpu.SemaphoreType.DMA((count,)),
            pltpu.SemaphoreType.DMA,
            pltpu.SemaphoreType.DMA,
        ],
        compiler_params=pltpu.CompilerParams(vmem_limit_bytes=60 * MIB),
        cost_estimate=pl.CostEstimate(
            flops=5 * 10**9, bytes_accessed=2 * share * depth, transcendentals=0
        ),
        name="parcel",
    )(states, rows, cols)


def code_base_kernel(
    scales_hbm, states_hbm, codes_hbm, out_ref, states_ref, codes_ref, scales_ref,
    scale_sem, state_sems, code_sems,
):
    depth, width = codes_ref.shape
    cuts = chunk_cuts(depth)
    count = len(cuts) - 1
    ahead = 3

    def copies(k):
        span = pl.ds(cuts[k], cuts[k + 1] - cuts[k])
        return (
            pltpu.make_async_copy(states_hbm.at[:, span], states_ref.at[:, span], state_sems.at[k]),
            pltpu.make_async_copy(codes_hbm.at[span, :], codes_ref.at[span, :], code_sems.at[k]),
        )

    scale_copy = pltpu.make_async_copy(scales_hbm, scales_ref, scale_sem)
    scale_copy.start()
    for k in range(min(ahead, count)):
        for copy in copies(k):
            copy.start()
    scale_copy.wait()
    for k in range(count):
        if k + ahead < count:
            for copy in copies(k + ahead):
                copy.start()
        for copy in copies(k):
            copy.wait()
        rows = []
        for i in range(cuts[k], cuts[k + 1], BLK):
            cols = []
            for c in range(0, width, BLK):
                block = codes_ref[i : i + BLK, c : c + BLK].astype(jnp.float32)
                cols.append((block * scales_ref[c // BLK, i // BLK]).astype(jnp.bfloat16))
            rows.append(jnp.concatenate(cols, axis=1) if len(cols) > 1 else cols[0])
        weights = jnp.concatenate(rows, axis=0)
        part = jnp.dot(
            states_ref[:, cuts[k] : cuts[k + 1]], weights, preferred_element_type=jnp.float32
        )
        if k == 0:
            out_ref[...] = part
        else:
            out_ref[...] += part


def chunk_cuts(depth):
    unit = depth // 32
    cuts = [0]
    for size in (1, 3) + (4,) * 7:
        cuts.append(cuts[-1] + size * unit)
    return cuts


def code_base(states, codes, scales_t):
    tokens, depth = states.shape
    width = codes.shape[1]
    count = len(chunk_cuts(depth)) - 1
    vmem = pl.BlockSpec(memory_space=pltpu.VMEM)
    away = pl.BlockSpec(memory_space=pltpu.HBM)
    return pl.pallas_call(
        code_base_kernel,
        in_specs=[away, away, away],
        out_specs=vmem,
        out_shape=jax.ShapeDtypeStruct((tokens, width), jnp.float32),
        scratch_shapes=[
            pltpu.VMEM((tokens, depth), jnp.bfloat16),
            pltpu.VMEM((depth, width), jnp.bfloat16),
            pltpu.SMEM(scales_t.shape, jnp.float32),
            pltpu.SemaphoreType.DMA,
            pltpu.SemaphoreType.DMA((count,)),
            pltpu.SemaphoreType.DMA((count,)),
        ],
        compiler_params=pltpu.CompilerParams(vmem_limit_bytes=48 * MIB),
        cost_estimate=pl.CostEstimate(
            flops=2 * tokens * depth * width,
            bytes_accessed=2 * depth * (tokens + width),
            transcendentals=0,
        ),
        name="code_base",
    )(scales_t, states, codes)


def score_kernel(
    ranks_ref, arrived_ref, base_ref, readout_ref, out_ref, scaled_ref,
    half_ref, cols_ref, factor_ref, terms_ref,
):
    tokens, width = base_ref.shape
    cores, pairs, total = arrived_ref.shape
    share = tokens // cores
    width_share = col_share(width, cores)
    depth_share = total - width_share - 3 * share
    for k in range(width // width_share):
        cols_ref[:, k * width_share : (k + 1) * width_share] = arrived_ref[
            k, :, depth_share : depth_share + width_share
        ].astype(jnp.float32)
    parts = []
    for i in range(3):
        start = depth_share + width_share + i * share
        parts.append(
            jnp.concatenate(
                [arrived_ref[k, :, start : start + share] for k in range(cores)], axis=1
            )
        )
    split = jnp.concatenate(parts, axis=0)
    over_pairs = (((0,), (0,)), ((), ()))
    which = lax.broadcasted_iota(jnp.int32, (pairs, 128), 0)
    gap = jnp.zeros((pairs, 128), jnp.float32)
    for q in range(pairs):
        mine = (ranks_ref[q] - ranks_ref[q + pairs]).astype(jnp.float32)
        gap = jnp.where(which == q, mine, gap)
    pair_weight = gap / (2 * pairs - 1)
    scaled = (
        jnp.concatenate([pair_weight] * (width // 128), axis=1)
        * cols_ref[...] * (1.0 / math.sqrt(pairs))
    ).astype(jnp.bfloat16)
    scaled_ref[...] = scaled
    step = lax.dot_general(
        split, jnp.concatenate([scaled, scaled, scaled], axis=0), over_pairs,
        preferred_element_type=jnp.float32,
    )
    half_ref[...] = (base_ref[...] + STEP_SIZE * step) * 0.5
    group = min(pairs, 16)
    for first in range(0, pairs, group):
        at = lax.broadcasted_iota(jnp.int32, (3 * pairs, group * 128), 0)
        lane = lax.broadcasted_iota(jnp.int32, (3 * pairs, group * 128), 1)
        goal = first + lane // 128
        hit = (at == goal) | (at == goal + pairs) | (at == goal + 2 * pairs)
        pick = jnp.where(hit, 0.5 * SIGMA_NOISE, 0.0).astype(jnp.bfloat16)
        factor_ref[:, first * 128 : (first + group) * 128] = lax.dot_general(
            split, pick, over_pairs, preferred_element_type=jnp.float32
        )

    tile = min(512, width)
    zero = jnp.zeros((8, tile), jnp.float32)

    def eight(i):
        return pl.ds(pl.multiple_of(i * 8, 8), 8)

    def fold(value):
        lanes = value[:, 0:128]
        for j in range(1, tile // 128):
            lanes = lanes + value[:, j * 128 : (j + 1) * 128]
        return lanes

    for start in range(0, width, tile):
        span = slice(start, start + tile)
        readout = jnp.broadcast_to(readout_ref[:, span], (8, tile))

        def rest_step(i, acc):
            u = half_ref[eight(i), span]
            return acc + u * jnp.tanh(u)

        rest = lax.fori_loop(0, tokens // 8, rest_step, zero, unroll=64)

        def one_pair(p, carry):
            col = jnp.broadcast_to(cols_ref[pl.ds(p, 1), span], (8, tile))
            lanes = pl.ds(pl.multiple_of(p * 128, 128), 128)

            def step(i, acc):
                plus, minus, total = acc
                factor = factor_ref[eight(i), lanes]
                u = half_ref[eight(i), span]
                shift = jnp.concatenate([factor] * (tile // 128), axis=1) * col
                up = u + shift
                um = u - shift
                return plus + up * jnp.tanh(up), minus + um * jnp.tanh(um), total + factor

            plus, minus, total = lax.fori_loop(
                0, tokens // 8, step, (zero, zero, jnp.zeros((8, 128), jnp.float32)),
                unroll=64,
            )
            linear = col * jnp.concatenate([total] * (tile // 128), axis=1)
            plus = fold((plus - rest + linear) * readout)
            minus = fold((minus - rest - linear) * readout)
            if start > 0:
                plus += terms_ref[eight(p), :]
                minus += terms_ref[eight(p + pairs), :]
            terms_ref[eight(p), :] = plus
            terms_ref[eight(p + pairs), :] = minus
            return carry

        lax.fori_loop(0, pairs, one_pair, 0, unroll=2)
    sums = jnp.sum(terms_ref[...].reshape(2 * pairs, 8, 128), axis=1)
    sums = jnp.sum(sums.T, axis=0, keepdims=True)
    out_ref[...] = jnp.broadcast_to(sums, out_ref.shape)


def score_sums(ranks, arrived, base, readout, copies):
    tokens, width = base.shape
    pairs = arrived.shape[1]
    vmem = pl.BlockSpec(memory_space=pltpu.VMEM)
    return pl.pallas_call(
        score_kernel,
        in_specs=[pl.BlockSpec(memory_space=pltpu.SMEM), vmem, vmem, vmem],
        out_specs=(vmem, vmem),
        out_shape=(
            jax.ShapeDtypeStruct((copies, 2 * pairs), jnp.float32),
            jax.ShapeDtypeStruct((pairs, width), jnp.bfloat16),
        ),
        scratch_shapes=[
            pltpu.VMEM((tokens, width), jnp.float32),
            pltpu.VMEM((pairs, width), jnp.float32),
            pltpu.VMEM((tokens, pairs * 128), jnp.float32),
            pltpu.VMEM((2 * pairs * 8, 128), jnp.float32),
        ],
        compiler_params=pltpu.CompilerParams(vmem_limit_bytes=20 * MIB + 512 * pairs * tokens),
        cost_estimate=pl.CostEstimate(
            flops=14 * tokens * width * pairs,
            bytes_accessed=4 * tokens * width,
            transcendentals=2 * tokens * width * pairs,
        ),
        name="score_sums",
    )(ranks, arrived, base, readout)


def direction_kernel(arrived_ref, scaled_ref, out_hbm, block_ref, sems):
    slots, block, _ = block_ref.shape
    depth = out_hbm.shape[0]
    cores = arrived_ref.shape[0]
    scaled = scaled_ref[...]

    half = block // 2
    cuts = [0, half] + list(range(block, depth + 1, block))
    count = len(cuts) - 1
    share = depth // cores

    def copy(i):
        size = cuts[i + 1] - cuts[i]
        return pltpu.make_async_copy(
            block_ref.at[i % slots, pl.ds(0, size), :],
            out_hbm.at[pl.ds(cuts[i], size), :],
            sems.at[i % slots],
        )

    for i in range(count):
        if i >= slots:
            copy(i - slots).wait()
        start, size = cuts[i] % share, cuts[i + 1] - cuts[i]
        block_ref[i % slots, :size, :] = lax.dot_general(
            arrived_ref[cuts[i] // share, :, start : start + size], scaled,
            (((0,), (0,)), ((), ())), preferred_element_type=jnp.float32,
        ).astype(jnp.bfloat16)
        copy(i).start()
    for i in range(count - slots, count):
        copy(i).wait()


def make_direction(arrived, scaled, depth):
    pairs, width = scaled.shape
    block, slots = 1024, 4
    vmem = pl.BlockSpec(memory_space=pltpu.VMEM)
    return pl.pallas_call(
        direction_kernel,
        in_specs=[vmem, vmem],
        out_specs=pl.BlockSpec(memory_space=pltpu.HBM),
        out_shape=jax.ShapeDtypeStruct((depth, width), jnp.bfloat16),
        scratch_shapes=[
            pltpu.VMEM((slots, block, width), jnp.bfloat16),
            pltpu.SemaphoreType.DMA((slots,)),
        ],
        compiler_params=pltpu.CompilerParams(vmem_limit_bytes=32 * MIB),
        cost_estimate=pl.CostEstimate(
            flops=2 * pairs * depth * width, bytes_accessed=2 * depth * width, transcendentals=0
        ),
        name="direction",
    )(arrived, scaled)


def solution(mesh):
    pop, mp = mesh.shape["pop"], mesh.shape["mp"]

    def per_device(prompt_states, weight_codes, block_scales, readout, noise_rows, noise_cols, ranks):
        depth = weight_codes.shape[0]
        own = noise_rows.shape[0]
        parcel = make_parcel(prompt_states, noise_rows, noise_cols, pop * mp, mp)
        arrived = lax.all_to_all(parcel, ("mp", "pop"), split_axis=0, concat_axis=0, tiled=True)
        arrived = arrived.reshape(mp, pop * own, parcel.shape[2])

        base = code_base(prompt_states, weight_codes, block_scales.T)

        sums, scaled = score_sums(ranks, arrived, base, readout[None, :], pop * mp)
        everyone = lax.all_to_all(
            sums[:, None, :], ("pop", "mp"), split_axis=0, concat_axis=0, tiled=True
        )
        direction = make_direction(arrived, scaled, depth)
        scores = jnp.sum(everyone, axis=(0, 1)) * (1.0 / math.sqrt(TOK * FF))
        return (direction, scores)

    in_specs = (
        P("parts", None),
        P(None, ("pop", "mp")),
        P(None, ("pop", "mp")),
        P(("pop", "mp")),
        P(("parts", "pop"), None),
        P(("parts", "pop"), None),
        P("parts"),
    )
    out_specs = (P("parts", ("pop", "mp")), P("parts"))
    return jax.shard_map(
        per_device, mesh=mesh, in_specs=in_specs, out_specs=out_specs, check_vma=False
    )
```
